256 devices in a mesh: row: 32 (over x_hi, z, core), feat: 8 (over y, x_lo).
Axes of the slice: x: 4 (x_hi: 2, x_lo: 2; x = x_hi * 2 + x_lo), y: 4, z: 8, core: 2. Of those that a mesh axis runs over, the one named last changes fastest.
Arguments:
- bin_index: int32 [1024, 98304], P('feat', 'row'), may hold values from 0 to 63
- gradient: bfloat16 [32, 98304], P(None, ('row', 'feat')), may hold values from -6 to 6
- hessian: bfloat16 [98304], P(('row', 'feat')), may hold values from 0.25 to 4
- row_node: int32 [98304], P('row'), may hold values from 0 to 7
Outputs:
- split_gain: float32 [1024, 512], P(('feat', 'row'))
- best_gain: float32 [8], replicated
The draws below stay inside these ranges and needn't reach their ends.
All inputs are finite; a program needn't handle non-finite values.
Results may differ from the reference program's by a relative error of at most 0.0003.
Values may be sent and summed in bfloat16 or wider, within the bound.
No kernel may reach another device: no remote copies, remote signals or barrier semaphores. Data moves between devices by JAX's collectives and lax.ppermute only.
A program may use at most 128 MiB of HBM per device.

```python
import math
import jax
import jax.numpy as jnp
from jax import lax

FEATURES = 1024
OUTPUTS = 32
BINS = 64
NODES = 8
ROWS = 98304


def plant(values, stream_key, smallest, high):
    place = [jax.random.randint(jax.random.fold_in(stream_key, axis), (), 0, length) for axis, length in enumerate(values.shape)]
    longest = values.shape.index(max(values.shape))
    beside = place[:longest] + [(place[longest] + 1) % values.shape[longest]] + place[longest + 1:]
    return values.at[tuple(place)].set(smallest).at[tuple(beside)].set(high)


def steps_of(key, dims, split, smallest, high):
    loudness, own = 1.0, jax.random.fold_in(key, 6)
    for position, blocks in split:
        draws = jnp.exp(jax.random.uniform(jax.random.fold_in(own, position), (blocks,), jnp.float32, smallest / len(split), high / len(split)))
        loudness = loudness * jnp.repeat(draws, dims[position] // blocks).reshape([-1 if axis == position else 1 for axis in range(len(dims))])
    return loudness


def normal_values(stream_key, extent, deviation, limit, split=(), held_as=jnp.bfloat16):
    values = jax.random.normal(stream_key, extent, jnp.float32) * deviation
    if len(split) > 0:
        values = steps_of(stream_key, extent, split, -0.22, 0.18) * values
    return jnp.clip(values, min=-limit, max=limit).astype(held_as)


def setup_inputs(seed: int = 0) -> dict:
    key_list = jax.random.split(jax.random.key(seed), 5)
    bin_index = plant(jax.random.randint(key_list[0], (FEATURES, ROWS), 0, BINS), jax.random.fold_in(key_list[0], 1), 0, BINS - 1).astype(jnp.int32)
    gradient = normal_values(key_list[1], (OUTPUTS, ROWS), 1.0, 6.0, ((1, 256),))
    hessian = jnp.clip(jnp.exp(math.log(4.0) - 2.7725887 * jax.random.uniform(key_list[2], (ROWS,), jnp.float32) ** steps_of(key_list[2], (ROWS,), ((0, 256),), -0.2, 0.2)), 0.25, 4.0).astype(jnp.bfloat16)
    row_node = plant(jax.random.randint(key_list[3], (ROWS,), 0, NODES), jax.random.fold_in(key_list[3], 1), 0, NODES - 1).astype(jnp.int32)
    return {"bin_index": bin_index, "gradient": gradient, "hessian": hessian, "row_node": row_node}


ridge_term = 1.0


def score_splits(histogram, whole_sums):
    left_sums = jnp.cumsum(histogram, axis=1)
    right_sums = whole_sums - left_sums

    def part_score(sums):
        return jnp.sum(sums[..., :-1] * sums[..., :-1], axis=-1) / (sums[..., -1] + ridge_term)

    outputs_count = histogram.shape[-1] - 1
    score_terms = part_score(left_sums) + part_score(right_sums) - part_score(whole_sums)
    return jnp.transpose((0.5 / outputs_count) * score_terms, (0, 2, 1))


def reference(bin_index, gradient, hessian, row_node):
    stacked = jnp.concatenate([gradient, hessian[None, :]], 0)
    stacked_rows = stacked.astype(jnp.float32).T
    node_ids = row_node.astype(jnp.int32)
    node_totals = jax.ops.segment_sum(stacked_rows, node_ids, num_segments=NODES)

    def one_feature(feature_bins):
        cell_ids = (node_ids * BINS + feature_bins.astype(jnp.int32)).astype(jnp.int32)
        sums = jax.ops.segment_sum(stacked_rows, cell_ids, num_segments=NODES * BINS)
        return jnp.transpose(sums.reshape(NODES, BINS, -1), (1, 0, 2))

    histogram = lax.map(one_feature, bin_index)
    split_gain = score_splits(histogram, node_totals[None, None])
    best_gain = jnp.max(split_gain, axis=(0, 2))
    return split_gain.reshape(FEATURES, NODES * BINS), best_gain
```

```python
import jax
import jax.numpy as jnp
from jax import lax
from jax.experimental import pallas as pl
from jax.experimental.pallas import tpu as pltpu
from jax.sharding import Mesh
from jax.sharding import PartitionSpec as P

BINS = 64
NODES = 8
OUTPUTS = 32
OWNED = 4
LANES = OWNED * BINS
GRAD_ROWS = NODES * OUTPUTS
SUM_ROWS = GRAD_ROWS + NODES
WIRE_ROWS = GRAD_ROWS + 4 * NODES
STEPS = 8.0
TOP = 32000.0
HESS_UNIT = 512.0
HESS_SPLIT = 4096.0
ROW = ("xh", "z", "c")
FEAT = ("y", "xl")
ALL = ROW + FEAT
NEAR = ("xh", "c", "y", "xl")
f32 = jnp.float32
bf16 = jnp.bfloat16

ridge_term = 1.0


def hist_kernel(place, pay, b00, b01, b10, b11, out, masked):
    row_shards = (b00, b01, b10, b11)
    shard_rows = b00.shape[-1]
    columns = pay.shape[0] // 4
    blocks = shard_rows // columns // 128

    @pl.when(pl.program_id(0) == 0)
    def _():
        node_of_row = lax.broadcasted_iota(jnp.int32, (16, 128), 0).astype(f32).astype(bf16)
        for r in range(4):
            group = (place[0] ^ (r // 2)) * 2 + (place[1] ^ (r % 2))

            def fill(s, carry, r=r, group=group):
                shard = group * columns + s
                for i in range(blocks):
                    at = pl.multiple_of(r * shard_rows + s * (blocks * 128) + i * 128, 128)
                    grad = pay[shard, OUTPUTS * i : OUTPUTS * (i + 1), :]
                    first = OUTPUTS * blocks
                    hess = jnp.broadcast_to(pay[shard, first + i : first + i + 1, :], (16, 128))
                    first = first + blocks
                    node = pay[shard, first + i : first + i + 1, :]
                    wide = jnp.broadcast_to(node, (OUTPUTS, 128))
                    for n in range(NODES):
                        masked[OUTPUTS * n : OUTPUTS * (n + 1), pl.ds(at, 128)] = jnp.where(
                            wide == jnp.array(n, bf16), grad, jnp.zeros_like(grad)
                        )
                    masked[GRAD_ROWS : GRAD_ROWS + 16, pl.ds(at, 128)] = jnp.where(
                        jnp.broadcast_to(node, (16, 128)) == node_of_row,
                        hess,
                        jnp.zeros_like(hess),
                    )
                return carry

            lax.fori_loop(0, columns, fill, 0)

    level = lax.broadcasted_iota(jnp.int32, (BINS, shard_rows), 0).astype(f32).astype(bf16)
    sections = []
    for ref in row_shards:
        parts = [
            jnp.where(
                jnp.broadcast_to(ref[0, f : f + 1, :], (BINS, shard_rows)) <= level,
                jnp.array(1, bf16),
                jnp.array(0, bf16),
            )
            for f in range(OWNED)
        ]
        sections.append(jnp.concatenate(parts, axis=0))
    upto = jnp.concatenate(sections, axis=1)
    sums = lax.dot_general(
        masked[0:SUM_ROWS, :], upto, (((1,), (1,)), ((), ())), preferred_element_type=f32
    )
    grads = sums[0:GRAD_ROWS].reshape(NODES, OUTPUTS, LANES)
    largest = jnp.max(jnp.abs(grads), axis=1)
    octave = jnp.ceil(jnp.log2(jnp.maximum(largest, 1e-30)) * STEPS + 0.01)
    factor = TOP * jnp.exp2(octave * (-1.0 / STEPS))
    scaled = jnp.floor(grads * factor[:, None, :] + 0.5).reshape(GRAD_ROWS, LANES)
    out[0, 0:GRAD_ROWS, :] = scaled.astype(jnp.int32).astype(jnp.int16)
    units = sums[GRAD_ROWS:SUM_ROWS] * HESS_UNIT
    high = jnp.floor(units * (1.0 / HESS_SPLIT))
    low = units - high * HESS_SPLIT
    rest = jnp.concatenate([octave, high, low, jnp.zeros_like(low)], axis=0)
    out[0, GRAD_ROWS:WIRE_ROWS, :] = rest.astype(jnp.int32).astype(jnp.int16)


def local_sums(place, pay, pieces):
    blocks, owned, shard_rows = pieces[0].shape
    bins_spec = pl.BlockSpec((1, owned, shard_rows), lambda j, place: (j, 0, 0))
    return pl.pallas_call(
        hist_kernel,
        out_shape=jax.ShapeDtypeStruct((blocks, WIRE_ROWS, LANES), jnp.int16),
        grid_spec=pltpu.PrefetchScalarGridSpec(
            num_scalar_prefetch=1,
            grid=(blocks,),
            in_specs=[pl.BlockSpec(pay.shape, lambda j, place: (0, 0, 0))] + [bins_spec] * 4,
            out_specs=pl.BlockSpec((1, WIRE_ROWS, LANES), lambda j, place: (j, 0, 0)),
            scratch_shapes=[pltpu.VMEM((GRAD_ROWS + 16, 4 * shard_rows), bf16)],
        ),
        compiler_params=pltpu.CompilerParams(vmem_limit_bytes=56 << 20),
        name="left_sums",
    )(place, pay, *pieces)


def score_kernel(devices, parts, gain_out, best_out):
    left = jnp.zeros((NODES, OUTPUTS, LANES), f32)
    left_hess = jnp.zeros((NODES, LANES), f32)
    for s in range(parts.shape[0]):
        scaled = parts[s, 0:GRAD_ROWS, :].astype(jnp.int32).astype(f32)
        rest = parts[s, GRAD_ROWS:WIRE_ROWS, :].astype(jnp.int32).astype(f32)
        unit = jnp.exp2(rest[0:NODES] * (1.0 / STEPS)) * (1.0 / TOP)
        left = left + scaled.reshape(NODES, OUTPUTS, LANES) * unit[:, None, :]
        left_hess = left_hess + (
            rest[NODES : 2 * NODES] * HESS_SPLIT + rest[2 * NODES : 3 * NODES]
        ) * (1.0 / HESS_UNIT)
    whole = left[:, :, LANES - 1 :]
    whole_hess = left_hess[:, LANES - 1 :]
    right = whole - left
    right_hess = whole_hess - left_hess

    def part_score(sums, hess):
        return jnp.sum(sums * sums, axis=1) / (hess + ridge_term)

    terms = part_score(left, left_hess) + part_score(right, right_hess)
    gain = (0.5 / OUTPUTS) * (terms - part_score(whole, whole_hess))
    for f in range(OWNED):
        for n in range(NODES):
            gain_out[f : f + 1, n * BINS : (n + 1) * BINS] = gain[
                n : n + 1, f * BINS : (f + 1) * BINS
            ]
    best = jnp.max(gain, axis=1, keepdims=True)
    sublane = lax.broadcasted_iota(jnp.int32, (NODES, 128), 0)
    lane = lax.broadcasted_iota(jnp.int32, (NODES, 128), 1)
    turned = jnp.max(jnp.where(sublane == lane, best, -jnp.inf), axis=0, keepdims=True)
    best_out[...] = jnp.broadcast_to(turned[:, 0:NODES], (devices, NODES))


def final_scores(parts, devices):
    return pl.pallas_call(
        lambda *refs: score_kernel(devices, *refs),
        out_shape=(
            jax.ShapeDtypeStruct((OWNED, NODES * BINS), f32),
            jax.ShapeDtypeStruct((devices, NODES), f32),
        ),
        compiler_params=pltpu.CompilerParams(vmem_limit_bytes=48 << 20),
        name="split_scores",
    )(parts)


def on_device(bin_index, gradient, hessian, row_node):
    xh, c = lax.axis_index("xh"), lax.axis_index("c")
    shard_rows = bin_index.shape[1]
    depth = lax.axis_size("z")
    table = bin_index.reshape(2, depth, 2, OWNED, shard_rows)
    pieces = []
    for r in range(4):
        piece = lax.dynamic_index_in_dim(table, xh ^ (r // 2), 0, keepdims=False)
        piece = lax.dynamic_index_in_dim(piece, c ^ (r % 2), 1, keepdims=False)
        pieces.append(piece.astype(bf16))
    pieces[1] = lax.ppermute(pieces[1], "c", [(0, 1), (1, 0)])
    pieces[2] = lax.ppermute(pieces[2], "xh", [(0, 1), (1, 0)])
    pieces[3] = lax.ppermute(pieces[3], ("xh", "c"), [(0, 3), (1, 2), (2, 1), (3, 0)])

    own_rows = gradient.shape[1]
    blocks = own_rows // 128
    nodes = lax.dynamic_slice_in_dim(row_node, lax.axis_index(FEAT) * own_rows, own_rows, 0)
    pay = jnp.concatenate(
        [gradient[:, 128 * i : 128 * (i + 1)] for i in range(blocks)]
        + [hessian.reshape(blocks, 128), nodes.astype(bf16).reshape(blocks, 128)],
        axis=0,
    )
    pay = jnp.pad(pay, ((0, -pay.shape[0] % 8), (0, 0)))
    near = lax.axis_size(NEAR)
    pay = lax.all_to_all(jnp.broadcast_to(pay[None], (near,) + pay.shape), NEAR, 0, 0, tiled=True)

    place = jnp.stack([xh, c]).astype(jnp.int32)
    sums = local_sums(place, pay, pieces)
    parts = lax.all_to_all(sums, "z", 0, 0, tiled=True)
    gain, best = final_scores(parts, lax.axis_size(ALL))
    best = lax.all_to_all(best, ALL, 0, 0, tiled=True)
    return gain, jnp.max(best, axis=0)


def solution(mesh):
    split = Mesh(mesh.devices.reshape(2, 8, 2, 4, 2), ALL)
    in_specs = (P(FEAT, ROW), P(None, ROW + FEAT), P(ROW + FEAT), P(ROW))
    out_specs = (P(FEAT + ROW, None), P())
    return jax.shard_map(
        on_device, mesh=split, in_specs=in_specs, out_specs=out_specs, check_vma=False
    )
```

```python
import jax
import jax.numpy as jnp
from jax import lax
from jax.experimental import pallas as pl
from jax.experimental.pallas import tpu as pltpu
from jax.sharding import Mesh
from jax.sharding import PartitionSpec as P

BINS = 64
NODES = 8
OUTPUTS = 32
OWNED = 4
LANES = OWNED * BINS
GRAD_ROWS = NODES * OUTPUTS
SUM_ROWS = GRAD_ROWS + NODES
WIRE_ROWS = GRAD_ROWS + 4 * NODES
STEPS = 8.0
TOP = 32000.0
HESS_UNIT = 512.0
HESS_SPLIT = 4096.0
ROW = ("xh", "zh", "zl", "c")
FEAT = ("y", "xl")
ALL = ROW + FEAT
NEAR = ("xh", "zl", "y", "xl")
f32 = jnp.float32
bf16 = jnp.bfloat16

ridge_term = 1.0


def prep_kernel(place, bins, grad, hess, nodes, own, other, pay):
    c, column = place[2], place[3]
    blocks = grad.shape[1] // 128
    for t in range(bins.shape[0] // (2 * OWNED)):
        both = bins[t * 2 * OWNED : (t + 1) * 2 * OWNED, :].astype(f32)
        first, second = both[0:OWNED], both[OWNED : 2 * OWNED]
        own[t] = jnp.where(c == 0, first, second).astype(bf16)
        other[t] = jnp.where(c == 0, second, first).astype(bf16)
    node = nodes[0:blocks, :]
    for s in range(1, nodes.shape[0] // blocks):
        node = jnp.where(column == s, nodes[s * blocks : (s + 1) * blocks, :], node)
    rest = jnp.concatenate(
        [
            hess[...].astype(f32),
            node.astype(f32),
            jnp.zeros((pay.shape[1] - (OUTPUTS + 2) * blocks, 128), f32),
        ],
        axis=0,
    ).astype(bf16)
    grads = [grad[:, 128 * i : 128 * (i + 1)] for i in range(blocks)]

    def fill(s, carry):
        for i in range(blocks):
            pay[s, OUTPUTS * i : OUTPUTS * (i + 1), :] = grads[i]
        pay[s, OUTPUTS * blocks :, :] = rest
        return carry

    lax.fori_loop(0, pay.shape[0], fill, 0)


def prepare(place, bin_index, gradient, hessian, row_node, near):
    features, shard_rows = bin_index.shape
    blocks = gradient.shape[1] // 128
    groups = features // (2 * OWNED)
    pay_rows = OUTPUTS * blocks + -(-2 * blocks // 8) * 8
    return pl.pallas_call(
        prep_kernel,
        out_shape=(
            jax.ShapeDtypeStruct((groups, OWNED, shard_rows), bf16),
            jax.ShapeDtypeStruct((groups, OWNED, shard_rows), bf16),
            jax.ShapeDtypeStruct((near, pay_rows, 128), bf16),
        ),
        grid_spec=pltpu.PrefetchScalarGridSpec(num_scalar_prefetch=1),
        compiler_params=pltpu.CompilerParams(vmem_limit_bytes=32 << 20),
        name="prepare",
    )(place, bin_index, gradient, hessian.reshape(blocks, 128), row_node.reshape(-1, 128))


def sort_kernel(place, own, other, p0, p1, p2, p3):
    xh, zl = place[0], place[1]
    for r, out in enumerate((p0, p1, p2, p3)):
        for j in range(out.shape[1]):
            t = ((xh ^ (r // 2)) * out.shape[1] + j) * 2 + (zl ^ (r % 2))
            out[0, j] = own[t]
            out[1, j] = other[t]


def sort_by_neighbour(place, own, other):
    groups, owned, shard_rows = own.shape
    shape = jax.ShapeDtypeStruct((2, groups // 4, owned, shard_rows), bf16)
    return pl.pallas_call(
        sort_kernel,
        out_shape=(shape,) * 4,
        grid_spec=pltpu.PrefetchScalarGridSpec(num_scalar_prefetch=1),
        compiler_params=pltpu.CompilerParams(vmem_limit_bytes=32 << 20),
        name="sort_bins",
    )(place, own, other)


def hist_kernel(place, pay0, pay1, b0, b1, b2, b3, out, masked):
    shard_rows = b0.shape[-1]
    columns = pay0.shape[0] // 4
    blocks = shard_rows // columns // 128

    @pl.when(pl.program_id(0) == 0)
    def _():
        node_of_row = lax.broadcasted_iota(jnp.int32, (16, 128), 0).astype(f32).astype(bf16)
        for r in range(8):
            group = (place[0] ^ (r // 4)) * 2 + (place[1] ^ (r // 2 % 2))
            pay = (pay0, pay1)[r % 2]

            def fill(s, carry, r=r, group=group, pay=pay):
                shard = group * columns + s
                for i in range(blocks):
                    at = pl.multiple_of(r * shard_rows + s * (blocks * 128) + i * 128, 128)
                    grad = pay[shard, OUTPUTS * i : OUTPUTS * (i + 1), :]
                    first = OUTPUTS * blocks
                    hess = jnp.broadcast_to(pay[shard, first + i : first + i + 1, :], (16, 128))
                    first = first + blocks
                    node = pay[shard, first + i : first + i + 1, :]
                    wide = jnp.broadcast_to(node, (OUTPUTS, 128))
                    for n in range(NODES):
                        masked[OUTPUTS * n : OUTPUTS * (n + 1), pl.ds(at, 128)] = jnp.where(
                            wide == jnp.array(n, bf16), grad, jnp.zeros_like(grad)
                        )
                    masked[GRAD_ROWS : GRAD_ROWS + 16, pl.ds(at, 128)] = jnp.where(
                        jnp.broadcast_to(node, (16, 128)) == node_of_row,
                        hess,
                        jnp.zeros_like(hess),
                    )
                return carry

            lax.fori_loop(0, columns, fill, 0)

    level = lax.broadcasted_iota(jnp.int32, (BINS, shard_rows), 0).astype(f32).astype(bf16)
    sections = []
    for ref in (b0, b1, b2, b3):
        for half in range(2):
            parts = [
                jnp.where(
                    jnp.broadcast_to(ref[half, 0, f : f + 1, :], (BINS, shard_rows)) <= level,
                    jnp.array(1, bf16),
                    jnp.array(0, bf16),
                )
                for f in range(OWNED)
            ]
            sections.append(jnp.concatenate(parts, axis=0))
    upto = jnp.concatenate(sections, axis=1)
    sums = lax.dot_general(
        masked[0:SUM_ROWS, :], upto, (((1,), (1,)), ((), ())), preferred_element_type=f32
    )
    grads = sums[0:GRAD_ROWS].reshape(NODES, OUTPUTS, LANES)
    largest = jnp.max(jnp.abs(grads), axis=1)
    octave = jnp.ceil(jnp.log2(jnp.maximum(largest, 1e-30)) * STEPS + 0.01)
    factor = TOP * jnp.exp2(octave * (-1.0 / STEPS))
    scaled = jnp.floor(grads * factor[:, None, :] + 0.5).reshape(GRAD_ROWS, LANES)
    out[0, 0:GRAD_ROWS, :] = scaled.astype(jnp.int32).astype(jnp.int16)
    units = sums[GRAD_ROWS:SUM_ROWS] * HESS_UNIT
    high = jnp.floor(units * (1.0 / HESS_SPLIT))
    low = units - high * HESS_SPLIT
    rest = jnp.concatenate([octave, high, low, jnp.zeros_like(low)], axis=0)
    out[0, GRAD_ROWS:WIRE_ROWS, :] = rest.astype(jnp.int32).astype(jnp.int16)


def local_sums(place, pay0, pay1, pieces):
    halves, blocks, owned, shard_rows = pieces[0].shape
    bins_spec = pl.BlockSpec((halves, 1, owned, shard_rows), lambda j, place: (0, j, 0, 0))
    pay_spec = pl.BlockSpec(pay0.shape, lambda j, place: (0, 0, 0))
    return pl.pallas_call(
        hist_kernel,
        out_shape=jax.ShapeDtypeStruct((blocks, WIRE_ROWS, LANES), jnp.int16),
        grid_spec=pltpu.PrefetchScalarGridSpec(
            num_scalar_prefetch=1,
            grid=(blocks,),
            in_specs=[pay_spec] * 2 + [bins_spec] * 4,
            out_specs=pl.BlockSpec((1, WIRE_ROWS, LANES), lambda j, place: (j, 0, 0)),
            scratch_shapes=[pltpu.VMEM((GRAD_ROWS + 16, 8 * shard_rows), bf16)],
        ),
        compiler_params=pltpu.CompilerParams(vmem_limit_bytes=56 << 20),
        name="left_sums",
    )(place, pay0, pay1, *pieces)


def score_kernel(devices, parts, gain_out, best_out):
    left = jnp.zeros((NODES, OUTPUTS, LANES), f32)
    left_hess = jnp.zeros((NODES, LANES), f32)
    for s in range(parts.shape[0]):
        scaled = parts[s, 0:GRAD_ROWS, :].astype(jnp.int32).astype(f32)
        rest = parts[s, GRAD_ROWS:WIRE_ROWS, :].astype(jnp.int32).astype(f32)
        unit = jnp.exp2(rest[0:NODES] * (1.0 / STEPS)) * (1.0 / TOP)
        left = left + scaled.reshape(NODES, OUTPUTS, LANES) * unit[:, None, :]
        left_hess = left_hess + (
            rest[NODES : 2 * NODES] * HESS_SPLIT + rest[2 * NODES : 3 * NODES]
        ) * (1.0 / HESS_UNIT)
    whole = left[:, :, LANES - 1 :]
    whole_hess = left_hess[:, LANES - 1 :]
    right = whole - left
    right_hess = whole_hess - left_hess

    def part_score(sums, hess):
        return jnp.sum(sums * sums, axis=1) / (hess + ridge_term)

    terms = part_score(left, left_hess) + part_score(right, right_hess)
    gain = (0.5 / OUTPUTS) * (terms - part_score(whole, whole_hess))
    for f in range(OWNED):
        for n in range(NODES):
            gain_out[f : f + 1, n * BINS : (n + 1) * BINS] = gain[
                n : n + 1, f * BINS : (f + 1) * BINS
            ]
    best = jnp.max(gain, axis=1, keepdims=True)
    sublane = lax.broadcasted_iota(jnp.int32, (NODES, 128), 0)
    lane = lax.broadcasted_iota(jnp.int32, (NODES, 128), 1)
    turned = jnp.max(jnp.where(sublane == lane, best, -jnp.inf), axis=0, keepdims=True)
    best_out[...] = jnp.broadcast_to(turned[:, 0:NODES], (devices, NODES))


def final_scores(parts, devices):
    return pl.pallas_call(
        lambda *refs: score_kernel(devices, *refs),
        out_shape=(
            jax.ShapeDtypeStruct((OWNED, NODES * BINS), f32),
            jax.ShapeDtypeStruct((devices, NODES), f32),
        ),
        compiler_params=pltpu.CompilerParams(vmem_limit_bytes=48 << 20),
        name="split_scores",
    )(parts)


def on_device(bin_index, gradient, hessian, row_node):
    place = jnp.stack([lax.axis_index("xh"), lax.axis_index("zl"), lax.axis_index("c"), lax.axis_index(FEAT)])
    swap = [(0, 1), (1, 0)]
    own, other, pay = prepare(place, bin_index, gradient, hessian, row_node, lax.axis_size(NEAR))
    other = lax.ppermute(other, "c", swap)
    pieces = list(sort_by_neighbour(place, own, other))
    pay = lax.all_to_all(pay, NEAR, 0, 0, tiled=True)
    pieces[1] = lax.ppermute(pieces[1], "zl", swap)
    pieces[2] = lax.ppermute(pieces[2], "xh", swap)
    pieces[3] = lax.ppermute(pieces[3], ("xh", "zl"), [(0, 3), (1, 2), (2, 1), (3, 0)])
    pay, pieces = lax.optimization_barrier((pay, pieces))
    pay_other = lax.ppermute(pay, "c", swap)
    sums = local_sums(place, pay, pay_other, pieces)
    parts = lax.all_to_all(sums, "zh", 0, 0, tiled=True)
    gain, best = final_scores(parts, lax.axis_size(ALL))
    best = lax.all_to_all(best, ALL, 0, 0, tiled=True)
    return gain, jnp.max(best, axis=0)


def solution(mesh):
    split = Mesh(mesh.devices.reshape(2, 4, 2, 2, 4, 2), ALL)
    in_specs = (P(FEAT, ROW), P(None, ROW + FEAT), P(ROW + FEAT), P(ROW))
    out_specs = (P(FEAT + ROW, None), P())
    return jax.shard_map(
        on_device, mesh=split, in_specs=in_specs, out_specs=out_specs, check_vma=False
    )
```

```python
import jax
import jax.numpy as jnp
from jax import lax
from jax.experimental import pallas as pl
from jax.experimental.pallas import tpu as pltpu
from jax.sharding import Mesh
from jax.sharding import PartitionSpec as P

BINS = 64
NODES = 8
OUTPUTS = 32
OWNED = 4
LANES = OWNED * BINS
GRAD_ROWS = NODES * OUTPUTS
SUM_ROWS = GRAD_ROWS + NODES
WIRE_ROWS = GRAD_ROWS + 4 * NODES
STEPS = 8.0
TOP = 32000.0
HESS_UNIT = 512.0
HESS_SPLIT = 4096.0
ROW = ("xh", "zh", "zl", "c")
FEAT = ("y", "xl")
ALL = ROW + FEAT
NEAR = ("xh", "zl", "y", "xl")
f32 = jnp.float32
bf16 = jnp.bfloat16

ridge_term = 1.0


def pay_kernel(place, grad_hbm, hess_hbm, nodes_hbm, pay, grad, hess, nodes, sems):
    copies = [
        pltpu.make_async_copy(src, dst, sems.at[i])
        for i, (src, dst) in enumerate(
            ((grad_hbm, grad), (hess_hbm, hess), (nodes_hbm, nodes))
        )
    ]
    for copy in copies:
        copy.start()
    for copy in copies:
        copy.wait()
    column = place[4]
    blocks = grad.shape[1] // 128
    node = nodes[0:blocks, :]
    for s in range(1, nodes.shape[0] // blocks):
        node = jnp.where(column == s, nodes[s * blocks : (s + 1) * blocks, :], node)
    rest = jnp.concatenate(
        [
            hess[...].astype(f32),
            node.astype(f32),
            jnp.zeros((pay.shape[1] - (OUTPUTS + 2) * blocks, 128), f32),
        ],
        axis=0,
    ).astype(bf16)
    grads = [grad[:, 128 * i : 128 * (i + 1)] for i in range(blocks)]
    for s in range(pay.shape[0]):
        for i in range(blocks):
            pay[s, OUTPUTS * i : OUTPUTS * (i + 1), :] = grads[i]
        pay[s, OUTPUTS * blocks :, :] = rest


def payload(place, gradient, hessian, row_node, near):
    blocks = gradient.shape[1] // 128
    pay_rows = OUTPUTS * blocks + -(-2 * blocks // 8) * 8
    hessian = hessian.reshape(blocks, 128)
    row_node = row_node.reshape(-1, 128)
    return pl.pallas_call(
        pay_kernel,
        out_shape=jax.ShapeDtypeStruct((near, pay_rows, 128), bf16),
        grid_spec=pltpu.PrefetchScalarGridSpec(
            num_scalar_prefetch=1,
            in_specs=[pl.BlockSpec(memory_space=pl.ANY)] * 3,
            scratch_shapes=[
                pltpu.VMEM(gradient.shape, bf16),
                pltpu.VMEM(hessian.shape, bf16),
                pltpu.VMEM(row_node.shape, jnp.int32),
                pltpu.SemaphoreType.DMA((3,)),
            ],
        ),
        name="payload",
    )(place, gradient, hessian, row_node)


def cut_kernel(place, bins_hbm, p0, p1, p2, p3, bins, sems):
    xh, zl, c = place[0], place[1], place[2]
    tile = 2 * OWNED
    part = bins.shape[0] // sems.shape[0]
    copies = [
        pltpu.make_async_copy(
            bins_hbm.at[i * part : (i + 1) * part], bins.at[i * part : (i + 1) * part], sems.at[i]
        )
        for i in range(sems.shape[0])
    ]
    for copy in copies:
        copy.start()
    for copy in copies:
        copy.wait()
    depth = p0.shape[1]
    for r, out in enumerate((p0, p1, p2, p3)):
        for j in range(depth):
            t = ((xh ^ (r // 2)) * depth + j) * 2 + (zl ^ (r % 2))
            both = bins[pl.ds(pl.multiple_of(t * tile, tile), tile), :].astype(f32)
            first, second = both[0:OWNED], both[OWNED:tile]
            out[0, j] = jnp.where(c == 0, first, second).astype(bf16)
            out[1, j] = jnp.where(c == 0, second, first).astype(bf16)


def cut_by_neighbour(place, bin_index):
    features, shard_rows = bin_index.shape
    shape = jax.ShapeDtypeStruct((2, features // (8 * OWNED), OWNED, shard_rows), bf16)
    return pl.pallas_call(
        cut_kernel,
        out_shape=(shape,) * 4,
        grid_spec=pltpu.PrefetchScalarGridSpec(
            num_scalar_prefetch=1,
            in_specs=[pl.BlockSpec(memory_space=pl.ANY)],
            scratch_shapes=[
                pltpu.VMEM(bin_index.shape, jnp.int32),
                pltpu.SemaphoreType.DMA((4,)),
            ],
        ),
        compiler_params=pltpu.CompilerParams(vmem_limit_bytes=32 << 20),
        name="cut_bins",
    )(place, bin_index)


def hist_kernel(place, *refs):
    pays, refs = refs[:1], refs[1:]
    pieces, refs = refs[:4], refs[4:]
    out, masked = refs
    columns = pays[0].shape[0] // 4
    blocks = pays[0].shape[1] // OUTPUTS
    run = columns * blocks * 128

    @pl.when(pl.program_id(0) == 0)
    def _():
        node_of_row = lax.broadcasted_iota(jnp.int32, (16, 128), 0).astype(f32).astype(bf16)
        for k, pay in enumerate(pays):
            for r in range(4):
                group = (place[0] ^ (r // 2)) * 2 + (place[1] ^ (r % 2))
                for s in range(columns):
                    shard = group * columns + s
                    for i in range(blocks):
                        at = (k * 4 + r) * run + (s * blocks + i) * 128
                        grad = pay[shard, OUTPUTS * i : OUTPUTS * (i + 1), :]
                        first = OUTPUTS * blocks
                        hess = jnp.broadcast_to(pay[shard, first + i : first + i + 1, :], (16, 128))
                        first = first + blocks
                        node = pay[shard, first + i : first + i + 1, :]
                        wide = jnp.broadcast_to(node, (OUTPUTS, 128))
                        for n in range(NODES):
                            masked[OUTPUTS * n : OUTPUTS * (n + 1), at : at + 128] = jnp.where(
                                wide == jnp.array(n, bf16), grad, jnp.zeros_like(grad)
                            )
                        masked[GRAD_ROWS : GRAD_ROWS + 16, at : at + 128] = jnp.where(
                            jnp.broadcast_to(node, (16, 128)) == node_of_row,
                            hess,
                            jnp.zeros_like(hess),
                        )

    level = lax.broadcasted_iota(jnp.int32, (BINS, run), 0).astype(f32).astype(bf16)
    sections = []
    for piece in pieces:
        rows = piece[0, 0]
        sections.append(
            jnp.concatenate(
                [
                    jnp.where(
                        jnp.broadcast_to(rows[f : f + 1, :], (BINS, run)) <= level,
                        jnp.array(1, bf16),
                        jnp.array(0, bf16),
                    )
                    for f in range(OWNED)
                ],
                axis=0,
            )
        )
    upto = jnp.concatenate(sections, axis=1)
    sums = lax.dot_general(
        masked[0:SUM_ROWS, :], upto, (((1,), (1,)), ((), ())), preferred_element_type=f32
    )
    out[0] = sums


def local_sums(place, core, pay, pieces):
    halves, blocks, owned, shard_rows = pieces[0].shape
    bins_spec = pl.BlockSpec((1, 1, owned, shard_rows), lambda j, place: (core, j, 0, 0))
    pay_spec = pl.BlockSpec(pay.shape, lambda j, place: (0, 0, 0))
    rows = 4 * shard_rows
    flops = 2 * SUM_ROWS * rows * LANES * blocks
    return pl.pallas_call(
        hist_kernel,
        out_shape=jax.ShapeDtypeStruct((blocks, SUM_ROWS, LANES), f32),
        grid_spec=pltpu.PrefetchScalarGridSpec(
            num_scalar_prefetch=1,
            grid=(blocks,),
            in_specs=[pay_spec] + [bins_spec] * 4,
            out_specs=pl.BlockSpec((1, SUM_ROWS, LANES), lambda j, place: (j, 0, 0)),
            scratch_shapes=[pltpu.VMEM((GRAD_ROWS + 16, rows), bf16)],
        ),
        cost_estimate=pl.CostEstimate(flops=2 * flops, bytes_accessed=1 << 21, transcendentals=0),
        compiler_params=pltpu.CompilerParams(vmem_limit_bytes=48 << 20),
        name="left_sums",
    )(place, pay, *pieces)


def wire_kernel(mine, theirs, out):
    sums = mine[0] + theirs[0]
    grads = sums[0:GRAD_ROWS].reshape(NODES, OUTPUTS, LANES)
    largest = jnp.max(jnp.abs(grads), axis=1)
    octave = jnp.ceil(jnp.log2(jnp.maximum(largest, 1e-30)) * STEPS + 0.01)
    factor = TOP * jnp.exp2(octave * (-1.0 / STEPS))
    scaled = jnp.floor(grads * factor[:, None, :] + 0.5).reshape(GRAD_ROWS, LANES)
    out[0, 0:GRAD_ROWS, :] = scaled.astype(jnp.int32).astype(jnp.int16)
    units = sums[GRAD_ROWS:SUM_ROWS] * HESS_UNIT
    high = jnp.floor(units * (1.0 / HESS_SPLIT))
    low = units - high * HESS_SPLIT
    rest = jnp.concatenate([octave, high, low, jnp.zeros_like(low)], axis=0)
    out[0, GRAD_ROWS:WIRE_ROWS, :] = rest.astype(jnp.int32).astype(jnp.int16)


def to_wire(mine, theirs):
    blocks = mine.shape[0]
    sums_spec = pl.BlockSpec((1, SUM_ROWS, LANES), lambda j: (j, 0, 0))
    return pl.pallas_call(
        wire_kernel,
        out_shape=jax.ShapeDtypeStruct((blocks, WIRE_ROWS, LANES), jnp.int16),
        grid=(blocks,),
        in_specs=[sums_spec] * 2,
        out_specs=pl.BlockSpec((1, WIRE_ROWS, LANES), lambda j: (j, 0, 0)),
        compiler_params=pltpu.CompilerParams(vmem_limit_bytes=24 << 20),
        name="to_wire",
    )(mine, theirs)


def score_kernel(devices, parts, gain_out, best_out):
    left = jnp.zeros((NODES, OUTPUTS, LANES), f32)
    left_hess = jnp.zeros((NODES, LANES), f32)
    for s in range(parts.shape[0]):
        scaled = parts[s, 0:GRAD_ROWS, :].astype(jnp.int32).astype(f32)
        rest = parts[s, GRAD_ROWS:WIRE_ROWS, :].astype(jnp.int32).astype(f32)
        unit = jnp.exp2(rest[0:NODES] * (1.0 / STEPS)) * (1.0 / TOP)
        left = left + scaled.reshape(NODES, OUTPUTS, LANES) * unit[:, None, :]
        left_hess = left_hess + (
            rest[NODES : 2 * NODES] * HESS_SPLIT + rest[2 * NODES : 3 * NODES]
        ) * (1.0 / HESS_UNIT)
    whole = left[:, :, LANES - 1 :]
    whole_hess = left_hess[:, LANES - 1 :]
    right = whole - left
    right_hess = whole_hess - left_hess

    def part_score(sums, hess):
        return jnp.sum(sums * sums, axis=1) / (hess + ridge_term)

    terms = part_score(left, left_hess) + part_score(right, right_hess)
    gain = (0.5 / OUTPUTS) * (terms - part_score(whole, whole_hess))
    for f in range(OWNED):
        for n in range(NODES):
            gain_out[f : f + 1, n * BINS : (n + 1) * BINS] = gain[
                n : n + 1, f * BINS : (f + 1) * BINS
            ]
    best = jnp.max(gain, axis=1, keepdims=True)
    sublane = lax.broadcasted_iota(jnp.int32, (NODES, 128), 0)
    lane = lax.broadcasted_iota(jnp.int32, (NODES, 128), 1)
    turned = jnp.max(jnp.where(sublane == lane, best, -jnp.inf), axis=0, keepdims=True)
    best_out[...] = jnp.broadcast_to(turned[:, 0:NODES], (devices, NODES))


def final_scores(parts, devices):
    return pl.pallas_call(
        lambda *refs: score_kernel(devices, *refs),
        out_shape=(
            jax.ShapeDtypeStruct((OWNED, NODES * BINS), f32),
            jax.ShapeDtypeStruct((devices, NODES), f32),
        ),
        compiler_params=pltpu.CompilerParams(vmem_limit_bytes=48 << 20),
        name="split_scores",
    )(parts)


def on_device(bin_index, gradient, hessian, row_node):
    place = jnp.stack([lax.axis_index(name) for name in ("xh", "zl", "c", "y", FEAT)])
    swap = [(0, 1), (1, 0)]
    pay = payload(place, gradient, hessian, row_node, lax.axis_size(NEAR))
    pay = lax.all_to_all(pay, NEAR, 0, 0, tiled=True)
    pieces = list(cut_by_neighbour(place, bin_index))
    pieces[1] = lax.ppermute(pieces[1], "zl", swap)
    pieces[2] = lax.ppermute(pieces[2], "xh", swap)
    pieces[3] = lax.ppermute(pieces[3], ("xh", "zl"), [(0, 3), (1, 2), (2, 1), (3, 0)])
    theirs = lax.ppermute(local_sums(place, 1, pay, pieces), "c", swap)
    sums = to_wire(local_sums(place, 0, pay, pieces), theirs)
    parts = lax.all_to_all(sums, "zh", 0, 0, tiled=True)
    gain, best = final_scores(parts, lax.axis_size(ALL))
    best = lax.all_to_all(best, ALL, 0, 0, tiled=True)
    return gain, jnp.max(best, axis=0)


def solution(mesh):
    split = Mesh(mesh.devices.reshape(2, 4, 2, 2, 4, 2), ALL)
    in_specs = (P(FEAT, ROW), P(None, ROW + FEAT), P(ROW + FEAT), P(ROW))
    out_specs = (P(FEAT + ROW, None), P())
    return jax.shard_map(
        on_device, mesh=split, in_specs=in_specs, out_specs=out_specs, check_vma=False
    )
```

```python
import jax
import jax.numpy as jnp
from jax import lax
from jax.experimental import pallas as pl
from jax.experimental.pallas import tpu as pltpu
from jax.sharding import Mesh
from jax.sharding import PartitionSpec as P

BINS = 64
NODES = 8
OUTPUTS = 32
OWNED = 4
LANES = OWNED * BINS
DEPTH = 256
GRAD_ROWS = NODES * OUTPUTS
SUM_ROWS = GRAD_ROWS + NODES
WIRE_ROWS = GRAD_ROWS + 4 * NODES
STEPS = 8.0
TOP = 32000.0
HESS_UNIT = 512.0
HESS_SPLIT = 4096.0
ROW = ("xh", "zh", "zl", "c")
FEAT = ("y", "xl")
ALL = ROW + FEAT
NEAR = ("xh", "zl", "y", "xl")
f32 = jnp.float32
bf16 = jnp.bfloat16

ridge_term = 1.0


def pay_kernel(grad_hbm, hess_hbm, nodes_hbm, pay, grad, hess, nodes, sems):
    copies = [
        pltpu.make_async_copy(src, dst, sems.at[i])
        for i, (src, dst) in enumerate(
            ((grad_hbm, grad), (hess_hbm, hess), (nodes_hbm, nodes))
        )
    ]
    for copy in copies:
        copy.start()
    for copy in copies:
        copy.wait()
    column = lax.axis_index(FEAT)
    blocks = grad.shape[1] // 128
    node = nodes[0:blocks, :]
    for s in range(1, nodes.shape[0] // blocks):
        node = jnp.where(column == s, nodes[s * blocks : (s + 1) * blocks, :], node)
    rest = jnp.concatenate(
        [
            hess[...].astype(f32),
            node.astype(f32),
            jnp.zeros((pay.shape[1] - (OUTPUTS + 2) * blocks, 128), f32),
        ],
        axis=0,
    ).astype(bf16)
    grads = [grad[:, 128 * i : 128 * (i + 1)] for i in range(blocks)]
    for s in range(pay.shape[0]):
        for i in range(blocks):
            pay[s, OUTPUTS * i : OUTPUTS * (i + 1), :] = grads[i]
        pay[s, OUTPUTS * blocks :, :] = rest


def payload(gradient, hessian, row_node, near):
    blocks = gradient.shape[1] // 128
    pay_rows = OUTPUTS * blocks + -(-2 * blocks // 8) * 8
    hessian = hessian.reshape(blocks, 128)
    row_node = row_node.reshape(-1, 128)
    return pl.pallas_call(
        pay_kernel,
        out_shape=jax.ShapeDtypeStruct((near, pay_rows, 128), bf16),
        in_specs=[pl.BlockSpec(memory_space=pl.ANY)] * 3,
        scratch_shapes=[
            pltpu.VMEM(gradient.shape, bf16),
            pltpu.VMEM(hessian.shape, bf16),
            pltpu.VMEM(row_node.shape, jnp.int32),
            pltpu.SemaphoreType.DMA((3,)),
        ],
        name="payload",
    )(gradient, hessian, row_node)


def cut_kernel(bins_hbm, p0, p1, p2, p3, bins, sems):
    xh, zl, c = lax.axis_index("xh"), lax.axis_index("zl"), lax.axis_index("c")
    tile = 2 * OWNED
    part = bins.shape[0] // sems.shape[0]
    copies = [
        pltpu.make_async_copy(
            bins_hbm.at[i * part : (i + 1) * part], bins.at[i * part : (i + 1) * part], sems.at[i]
        )
        for i in range(sems.shape[0])
    ]
    for copy in copies:
        copy.start()
    for copy in copies:
        copy.wait()
    depth = p0.shape[1]
    for r, out in enumerate((p0, p1, p2, p3)):
        for j in range(depth):
            t = ((xh ^ (r // 2)) * depth + j) * 2 + (zl ^ (r % 2))
            both = bins[pl.ds(pl.multiple_of(t * tile, tile), tile), :].astype(f32)
            first, second = both[0:OWNED], both[OWNED:tile]
            out[0, j] = jnp.where(c == 0, first, second).astype(bf16)
            out[1, j] = jnp.where(c == 0, second, first).astype(bf16)


def cut_by_neighbour(bin_index):
    features, shard_rows = bin_index.shape
    shape = jax.ShapeDtypeStruct((2, features // (8 * OWNED), OWNED, shard_rows), bf16)
    return pl.pallas_call(
        cut_kernel,
        out_shape=(shape,) * 4,
        in_specs=[pl.BlockSpec(memory_space=pl.ANY)],
        scratch_shapes=[
            pltpu.VMEM(bin_index.shape, jnp.int32),
            pltpu.SemaphoreType.DMA((4,)),
        ],
        compiler_params=pltpu.CompilerParams(vmem_limit_bytes=32 << 20),
        name="cut_bins",
    )(bin_index)


def sums_kernel(pay, b0, b1, b2, b3, out):
    blocks = out.shape[0]
    columns = pay.shape[0] // 4
    layers = pay.shape[1] // OUTPUTS
    tiles = b0.shape[-1] // DEPTH
    xh, zl = lax.axis_index("xh"), lax.axis_index("zl")

    def body(*sums):
        level = lax.broadcasted_iota(jnp.int32, (BINS, DEPTH), 0).astype(f32).astype(bf16)
        node_of_row = lax.broadcasted_iota(jnp.int32, (16, 128), 0).astype(f32).astype(bf16)
        one, zero = jnp.array(1, bf16), jnp.array(0, bf16)

        def by_node(group, layer):
            shard, i = group * columns + layer // layers, layer % layers
            grad = pay[shard, OUTPUTS * i : OUTPUTS * (i + 1), :]
            i = OUTPUTS * layers + i
            hess = jnp.broadcast_to(pay[shard, i : i + 1, :], (16, 128))
            i = i + layers
            node = jnp.broadcast_to(pay[shard, i : i + 1, :], (16, 128))
            rows = []
            for n in range(NODES):
                here = node == jnp.array(n, bf16)
                rows += [jnp.where(here, grad[k : k + 16], zero) for k in range(0, OUTPUTS, 16)]
            rows.append(jnp.where(node == node_of_row, hess, zero))
            return jnp.concatenate(rows, axis=0)

        def upto(bins):
            return jnp.concatenate(
                [
                    jnp.where(jnp.broadcast_to(bins[f : f + 1], (BINS, DEPTH)) <= level, one, zero)
                    for f in range(OWNED)
                ],
                axis=0,
            )

        for r, piece in enumerate((b0, b1, b2, b3)):
            group = (xh ^ (r // 2)) * 2 + (zl ^ (r % 2))
            for t in range(tiles):
                values = jnp.concatenate(
                    [by_node(group, t * (DEPTH // 128) + k) for k in range(DEPTH // 128)], axis=1
                )
                for j in range(0, blocks, 2):
                    slot = j // 2 % 2
                    for m in range(2):
                        bins = piece[0, j + m, :, t * DEPTH : (t + 1) * DEPTH]
                        pltpu.matmul_push_rhs(upto(bins), slot, m, transpose=True)
                    for m in range(2):
                        pltpu.matmul_acc_lhs(sums[j + m], values, load_staged_rhs=slot)
        for j in range(blocks):
            out[j] = pltpu.matmul_pop(sums[j])[0:SUM_ROWS]

    pl.run_scoped(body, *[pltpu.ACC(j % 2)((GRAD_ROWS + 16, LANES), f32) for j in range(blocks)])


def local_sums(core, pay, pieces):
    halves, blocks, owned, shard_rows = pieces[0].shape
    bins_spec = pl.BlockSpec((1, blocks, owned, shard_rows), lambda j: (core, 0, 0, 0))
    pay_spec = pl.BlockSpec(pay.shape, lambda j: (0, 0, 0))
    flops = 2 * SUM_ROWS * 4 * shard_rows * LANES * blocks
    return pl.pallas_call(
        sums_kernel,
        out_shape=jax.ShapeDtypeStruct((blocks, SUM_ROWS, LANES), f32),
        grid=(1,),
        in_specs=[pay_spec] + [bins_spec] * 4,
        out_specs=pl.BlockSpec((blocks, SUM_ROWS, LANES), lambda j: (0, 0, 0)),
        cost_estimate=pl.CostEstimate(flops=flops, bytes_accessed=1 << 21, transcendentals=0),
        compiler_params=pltpu.CompilerParams(vmem_limit_bytes=32 << 20),
        name="left_sums",
    )(pay, *pieces)


def wire_kernel(mine, theirs, out):
    sums = mine[0] + theirs[0]
    grads = sums[0:GRAD_ROWS].reshape(NODES, OUTPUTS, LANES)
    largest = jnp.max(jnp.abs(grads), axis=1)
    octave = jnp.ceil(jnp.log2(jnp.maximum(largest, 1e-30)) * STEPS + 0.01)
    factor = TOP * jnp.exp2(octave * (-1.0 / STEPS))
    scaled = jnp.floor(grads * factor[:, None, :] + 0.5).reshape(GRAD_ROWS, LANES)
    out[0, 0:GRAD_ROWS, :] = scaled.astype(jnp.int32).astype(jnp.int16)
    units = sums[GRAD_ROWS:SUM_ROWS] * HESS_UNIT
    high = jnp.floor(units * (1.0 / HESS_SPLIT))
    low = units - high * HESS_SPLIT
    rest = jnp.concatenate([octave, high, low, jnp.zeros_like(low)], axis=0)
    out[0, GRAD_ROWS:WIRE_ROWS, :] = rest.astype(jnp.int32).astype(jnp.int16)


def to_wire(mine, theirs):
    blocks = mine.shape[0]
    sums_spec = pl.BlockSpec((1, SUM_ROWS, LANES), lambda j: (j, 0, 0))
    return pl.pallas_call(
        wire_kernel,
        out_shape=jax.ShapeDtypeStruct((blocks, WIRE_ROWS, LANES), jnp.int16),
        grid=(blocks,),
        in_specs=[sums_spec] * 2,
        out_specs=pl.BlockSpec((1, WIRE_ROWS, LANES), lambda j: (j, 0, 0)),
        compiler_params=pltpu.CompilerParams(vmem_limit_bytes=24 << 20),
        name="to_wire",
    )(mine, theirs)


def score_kernel(devices, parts, gain_out, best_out):
    left = jnp.zeros((NODES, OUTPUTS, LANES), f32)
    left_hess = jnp.zeros((NODES, LANES), f32)
    for s in range(parts.shape[0]):
        scaled = parts[s, 0:GRAD_ROWS, :].astype(jnp.int32).astype(f32)
        rest = parts[s, GRAD_ROWS:WIRE_ROWS, :].astype(jnp.int32).astype(f32)
        unit = jnp.exp2(rest[0:NODES] * (1.0 / STEPS)) * (1.0 / TOP)
        left = left + scaled.reshape(NODES, OUTPUTS, LANES) * unit[:, None, :]
        left_hess = left_hess + (
            rest[NODES : 2 * NODES] * HESS_SPLIT + rest[2 * NODES : 3 * NODES]
        ) * (1.0 / HESS_UNIT)
    whole = left[:, :, LANES - 1 :]
    whole_hess = left_hess[:, LANES - 1 :]
    right = whole - left
    right_hess = whole_hess - left_hess

    def part_score(sums, hess):
        return jnp.sum(sums * sums, axis=1) / (hess + ridge_term)

    terms = part_score(left, left_hess) + part_score(right, right_hess)
    gain = (0.5 / OUTPUTS) * (terms - part_score(whole, whole_hess))
    for f in range(OWNED):
        for n in range(NODES):
            gain_out[f : f + 1, n * BINS : (n + 1) * BINS] = gain[
                n : n + 1, f * BINS : (f + 1) * BINS
            ]
    best = jnp.max(gain, axis=1, keepdims=True)
    sublane = lax.broadcasted_iota(jnp.int32, (NODES, 128), 0)
    lane = lax.broadcasted_iota(jnp.int32, (NODES, 128), 1)
    turned = jnp.max(jnp.where(sublane == lane, best, -jnp.inf), axis=0, keepdims=True)
    best_out[...] = jnp.broadcast_to(turned[:, 0:NODES], (devices, NODES))


def final_scores(parts, devices):
    return pl.pallas_call(
        lambda *refs: score_kernel(devices, *refs),
        out_shape=(
            jax.ShapeDtypeStruct((OWNED, NODES * BINS), f32),
            jax.ShapeDtypeStruct((devices, NODES), f32),
        ),
        compiler_params=pltpu.CompilerParams(vmem_limit_bytes=48 << 20),
        name="split_scores",
    )(parts)


def on_device(bin_index, gradient, hessian, row_node):
    swap = [(0, 1), (1, 0)]
    pay = payload(gradient, hessian, row_node, lax.axis_size(NEAR))
    pay = lax.all_to_all(pay, NEAR, 0, 0, tiled=True)
    pieces = list(cut_by_neighbour(bin_index))
    pieces[1] = lax.ppermute(pieces[1], "zl", swap)
    pieces[2] = lax.ppermute(pieces[2], "xh", swap)
    pieces[3] = lax.ppermute(pieces[3], ("xh", "zl"), [(0, 3), (1, 2), (2, 1), (3, 0)])
    theirs = lax.ppermute(local_sums(1, pay, pieces), "c", swap)
    sums = to_wire(local_sums(0, pay, pieces), theirs)
    parts = lax.all_to_all(sums, "zh", 0, 0, tiled=True)
    gain, best = final_scores(parts, lax.axis_size(ALL))
    best = lax.all_to_all(best, ALL, 0, 0, tiled=True)
    return gain, jnp.max(best, axis=0)


def solution(mesh):
    split = Mesh(mesh.devices.reshape(2, 4, 2, 2, 4, 2), ALL)
    in_specs = (P(FEAT, ROW), P(None, ROW + FEAT), P(ROW + FEAT), P(ROW))
    out_specs = (P(FEAT + ROW, None), P())
    return jax.shard_map(
        on_device, mesh=split, in_specs=in_specs, out_specs=out_specs, check_vma=False
    )
```

```python
import functools

import jax
import jax.numpy as jnp
from jax import lax
from jax.experimental import pallas as pl
from jax.experimental.pallas import tpu as pltpu
from jax.sharding import Mesh
from jax.sharding import PartitionSpec as P

BINS = 64
NODES = 8
OUTPUTS = 32
OWNED = 4
LANES = OWNED * BINS
DEPTH = 256
GRAD_ROWS = NODES * OUTPUTS
SUM_ROWS = GRAD_ROWS + NODES
WIRE_ROWS = GRAD_ROWS + 4 * NODES
STEPS = 8.0
TOP = 32000.0
HESS_UNIT = 512.0
HESS_SPLIT = 4096.0
ROW = ("xh", "zh", "zl", "c")
FEAT = ("y", "xl")
ALL = ROW + FEAT
NEAR = ("xh", "zl", "y", "xl")
f32 = jnp.float32
bf16 = jnp.bfloat16

ridge_term = 1.0


def pay_kernel(grad_hbm, hess_hbm, nodes_hbm, pay, grad, hess, nodes, sems):
    copies = [
        pltpu.make_async_copy(src, dst, sems.at[i])
        for i, (src, dst) in enumerate(
            ((grad_hbm, grad), (hess_hbm, hess), (nodes_hbm, nodes))
        )
    ]
    for copy in copies:
        copy.start()
    for copy in copies:
        copy.wait()
    column = lax.axis_index(FEAT)
    blocks = grad.shape[1] // 128
    node = nodes[0:blocks, :]
    for s in range(1, nodes.shape[0] // blocks):
        node = jnp.where(column == s, nodes[s * blocks : (s + 1) * blocks, :], node)
    rest = jnp.concatenate(
        [
            hess[...].astype(f32),
            node.astype(f32),
            jnp.zeros((pay.shape[1] - (OUTPUTS + 2) * blocks, 128), f32),
        ],
        axis=0,
    ).astype(bf16)
    grads = [grad[:, 128 * i : 128 * (i + 1)] for i in range(blocks)]
    for s in range(pay.shape[0]):
        for i in range(blocks):
            pay[s, OUTPUTS * i : OUTPUTS * (i + 1), :] = grads[i]
        pay[s, OUTPUTS * blocks :, :] = rest


def payload(gradient, hessian, row_node, near):
    blocks = gradient.shape[1] // 128
    pay_rows = OUTPUTS * blocks + -(-2 * blocks // 8) * 8
    hessian = hessian.reshape(blocks, 128)
    row_node = row_node.reshape(-1, 128)
    return pl.pallas_call(
        pay_kernel,
        out_shape=jax.ShapeDtypeStruct((near, pay_rows, 128), bf16),
        in_specs=[pl.BlockSpec(memory_space=pl.ANY)] * 3,
        scratch_shapes=[
            pltpu.VMEM(gradient.shape, bf16),
            pltpu.VMEM(hessian.shape, bf16),
            pltpu.VMEM(row_node.shape, jnp.int32),
            pltpu.SemaphoreType.DMA((3,)),
        ],
        name="payload",
    )(gradient, hessian, row_node)


def cut_kernel(bins_hbm, p0, p1, p2, p3, bins, sems):
    xh, zl, c = lax.axis_index("xh"), lax.axis_index("zl"), lax.axis_index("c")
    tile = 2 * OWNED
    part = bins.shape[0] // sems.shape[0]
    copies = [
        pltpu.make_async_copy(
            bins_hbm.at[i * part : (i + 1) * part], bins.at[i * part : (i + 1) * part], sems.at[i]
        )
        for i in range(sems.shape[0])
    ]
    for copy in copies:
        copy.start()
    for copy in copies:
        copy.wait()
    depth = p0.shape[1]
    for r, out in enumerate((p0, p1, p2, p3)):
        for j in range(depth):
            t = ((xh ^ (r // 2)) * depth + j) * 2 + (zl ^ (r % 2))
            both = bins[pl.ds(pl.multiple_of(t * tile, tile), tile), :].astype(f32)
            first, second = both[0:OWNED], both[OWNED:tile]
            out[0, j] = jnp.where(c == 0, first, second).astype(bf16)
            out[1, j] = jnp.where(c == 0, second, first).astype(bf16)


def cut_by_neighbour(bin_index):
    features, shard_rows = bin_index.shape
    shape = jax.ShapeDtypeStruct((2, features // (8 * OWNED), OWNED, shard_rows), bf16)
    return pl.pallas_call(
        cut_kernel,
        out_shape=(shape,) * 4,
        in_specs=[pl.BlockSpec(memory_space=pl.ANY)],
        scratch_shapes=[
            pltpu.VMEM(bin_index.shape, jnp.int32),
            pltpu.SemaphoreType.DMA((4,)),
        ],
        compiler_params=pltpu.CompilerParams(vmem_limit_bytes=32 << 20),
        name="cut_bins",
    )(bin_index)


def sums_kernel(order, pay, b0, b1, b2, b3, out):
    blocks = len(order)
    zh, depth = lax.axis_index("zh"), lax.axis_size("zh")
    columns = pay.shape[0] // 4
    layers = pay.shape[1] // OUTPUTS
    tiles = b0.shape[-1] // DEPTH
    xh, zl = lax.axis_index("xh"), lax.axis_index("zl")

    def body(*sums):
        level = lax.broadcasted_iota(jnp.int32, (BINS, DEPTH), 0).astype(f32).astype(bf16)
        node_of_row = lax.broadcasted_iota(jnp.int32, (16, 128), 0).astype(f32).astype(bf16)
        one, zero = jnp.array(1, bf16), jnp.array(0, bf16)

        def by_node(group, layer):
            shard, i = group * columns + layer // layers, layer % layers
            grad = pay[shard, OUTPUTS * i : OUTPUTS * (i + 1), :]
            i = OUTPUTS * layers + i
            hess = jnp.broadcast_to(pay[shard, i : i + 1, :], (16, 128))
            i = i + layers
            node = jnp.broadcast_to(pay[shard, i : i + 1, :], (16, 128))
            rows = []
            for n in range(NODES):
                here = node == jnp.array(n, bf16)
                rows += [jnp.where(here, grad[k : k + 16], zero) for k in range(0, OUTPUTS, 16)]
            rows.append(jnp.where(node == node_of_row, hess, zero))
            return jnp.concatenate(rows, axis=0)

        def upto(bins):
            return jnp.concatenate(
                [
                    jnp.where(jnp.broadcast_to(bins[f : f + 1], (BINS, DEPTH)) <= level, one, zero)
                    for f in range(OWNED)
                ],
                axis=0,
            )

        for r, piece in enumerate((b0, b1, b2, b3)):
            group = (xh ^ (r // 2)) * 2 + (zl ^ (r % 2))
            for t in range(tiles):
                values = jnp.concatenate(
                    [by_node(group, t * (DEPTH // 128) + k) for k in range(DEPTH // 128)], axis=1
                )
                for j in range(0, blocks, 2):
                    slot = j // 2 % 2
                    for m in range(2):
                        keeper = (zh + order[j + m]) % depth
                        bins = piece[0, keeper, :, t * DEPTH : (t + 1) * DEPTH]
                        pltpu.matmul_push_rhs(upto(bins), slot, m, transpose=True)
                    for m in range(2):
                        pltpu.matmul_acc_lhs(sums[j + m], values, load_staged_rhs=slot)
        for j in range(blocks):
            out[j] = pltpu.matmul_pop(sums[j])[0:SUM_ROWS]

    pl.run_scoped(body, *[pltpu.ACC(j % 2)((GRAD_ROWS + 16, LANES), f32) for j in range(blocks)])


def local_sums(core, order, pay, pieces):
    halves, depth, owned, shard_rows = pieces[0].shape
    blocks = len(order)
    bins_spec = pl.BlockSpec((1, depth, owned, shard_rows), lambda j: (core, 0, 0, 0))
    pay_spec = pl.BlockSpec(pay.shape, lambda j: (0, 0, 0))
    flops = 2 * SUM_ROWS * 4 * shard_rows * LANES * blocks
    return pl.pallas_call(
        functools.partial(sums_kernel, order),
        out_shape=jax.ShapeDtypeStruct((blocks, SUM_ROWS, LANES), f32),
        grid=(1,),
        in_specs=[pay_spec] + [bins_spec] * 4,
        out_specs=pl.BlockSpec((blocks, SUM_ROWS, LANES), lambda j: (0, 0, 0)),
        cost_estimate=pl.CostEstimate(flops=flops, bytes_accessed=1 << 21, transcendentals=0),
        compiler_params=pltpu.CompilerParams(vmem_limit_bytes=32 << 20),
        name="left_sums",
    )(pay, *pieces)


def wire_kernel(first, mine, theirs, *outs):
    for j, out in enumerate(outs):
        sums = mine[j] + theirs[first + j]
        grads = sums[0:GRAD_ROWS].reshape(NODES, OUTPUTS, LANES)
        largest = jnp.max(jnp.abs(grads), axis=1)
        octave = jnp.ceil(jnp.log2(jnp.maximum(largest, 1e-30)) * STEPS + 0.01)
        factor = TOP * jnp.exp2(octave * (-1.0 / STEPS))
        scaled = jnp.floor(grads * factor[:, None, :] + 0.5).reshape(GRAD_ROWS, LANES)
        out[0:GRAD_ROWS, :] = scaled.astype(jnp.int32).astype(jnp.int16)
        units = sums[GRAD_ROWS:SUM_ROWS] * HESS_UNIT
        high = jnp.floor(units * (1.0 / HESS_SPLIT))
        low = units - high * HESS_SPLIT
        rest = jnp.concatenate([octave, high, low, jnp.zeros_like(low)], axis=0)
        out[GRAD_ROWS:WIRE_ROWS, :] = rest.astype(jnp.int32).astype(jnp.int16)


def to_wire(first, mine, theirs):
    return pl.pallas_call(
        functools.partial(wire_kernel, first),
        out_shape=(jax.ShapeDtypeStruct((WIRE_ROWS, LANES), jnp.int16),) * mine.shape[0],
        compiler_params=pltpu.CompilerParams(vmem_limit_bytes=24 << 20),
        name="to_wire",
    )(mine, theirs)


def score_kernel(devices, *refs):
    parts, (gain_out, best_out) = refs[:-2], refs[-2:]
    left = jnp.zeros((NODES, OUTPUTS, LANES), f32)
    left_hess = jnp.zeros((NODES, LANES), f32)
    for part in parts:
        scaled = part[0:GRAD_ROWS, :].astype(jnp.int32).astype(f32)
        rest = part[GRAD_ROWS:WIRE_ROWS, :].astype(jnp.int32).astype(f32)
        unit = jnp.exp2(rest[0:NODES] * (1.0 / STEPS)) * (1.0 / TOP)
        left = left + scaled.reshape(NODES, OUTPUTS, LANES) * unit[:, None, :]
        left_hess = left_hess + (
            rest[NODES : 2 * NODES] * HESS_SPLIT + rest[2 * NODES : 3 * NODES]
        ) * (1.0 / HESS_UNIT)
    whole = left[:, :, LANES - 1 :]
    whole_hess = left_hess[:, LANES - 1 :]
    right = whole - left
    right_hess = whole_hess - left_hess

    def part_score(sums, hess):
        return jnp.sum(sums * sums, axis=1) / (hess + ridge_term)

    terms = part_score(left, left_hess) + part_score(right, right_hess)
    gain = (0.5 / OUTPUTS) * (terms - part_score(whole, whole_hess))
    for f in range(OWNED):
        for n in range(NODES):
            gain_out[f : f + 1, n * BINS : (n + 1) * BINS] = gain[
                n : n + 1, f * BINS : (f + 1) * BINS
            ]
    best = jnp.max(gain, axis=1, keepdims=True)
    sublane = lax.broadcasted_iota(jnp.int32, (NODES, 128), 0)
    lane = lax.broadcasted_iota(jnp.int32, (NODES, 128), 1)
    turned = jnp.max(jnp.where(sublane == lane, best, -jnp.inf), axis=0, keepdims=True)
    best_out[...] = jnp.broadcast_to(turned[:, 0:NODES], (devices, NODES))


def final_scores(parts, devices):
    return pl.pallas_call(
        functools.partial(score_kernel, devices),
        out_shape=(
            jax.ShapeDtypeStruct((OWNED, NODES * BINS), f32),
            jax.ShapeDtypeStruct((devices, NODES), f32),
        ),
        compiler_params=pltpu.CompilerParams(vmem_limit_bytes=48 << 20),
        name="split_scores",
    )(*parts)


def on_device(bin_index, gradient, hessian, row_node):
    swap = [(0, 1), (1, 0)]
    pay = payload(gradient, hessian, row_node, lax.axis_size(NEAR))
    pay = lax.all_to_all(pay, NEAR, 0, 0, tiled=True)
    pieces = list(cut_by_neighbour(bin_index))
    pieces[1] = lax.ppermute(pieces[1], "zl", swap)
    pieces[2] = lax.ppermute(pieces[2], "xh", swap)
    pieces[3] = lax.ppermute(pieces[3], ("xh", "zl"), [(0, 3), (1, 2), (2, 1), (3, 0)])
    depth = lax.axis_size("zh")

    def ahead(x, d):
        return lax.ppermute(x, "zh", [(i, (i + d) % depth) for i in range(depth)])

    theirs = lax.ppermute(local_sums(1, (2, 1, 3, 0), pay, pieces), "c", swap)
    two, one = to_wire(0, local_sums(0, (2, 1), pay, pieces), theirs)
    pay, two, one = lax.optimization_barrier((pay, two, one))
    two, one = ahead(two, 2), ahead(one, 1)
    three, own = to_wire(2, local_sums(0, (3, 0), pay, pieces), theirs)
    one, two, three = lax.optimization_barrier((one, two, three))
    parts = (own, one, ahead(three, 3), two)
    gain, best = final_scores(parts, lax.axis_size(ALL))
    best = lax.all_to_all(best, ALL, 0, 0, tiled=True)
    return gain, jnp.max(best, axis=0)


def solution(mesh):
    split = Mesh(mesh.devices.reshape(2, 4, 2, 2, 4, 2), ALL)
    in_specs = (P(FEAT, ROW), P(None, ROW + FEAT), P(ROW + FEAT), P(ROW))
    out_specs = (P(FEAT + ROW, None), P())
    return jax.shard_map(
        on_device, mesh=split, in_specs=in_specs, out_specs=out_specs, check_vma=False
    )
```

```python
import functools

import jax
import jax.numpy as jnp
from jax import lax
from jax.experimental import pallas as pl
from jax.experimental.pallas import tpu as pltpu
from jax.sharding import Mesh
from jax.sharding import PartitionSpec as P

BINS = 64
NODES = 8
OUTPUTS = 32
OWNED = 4
LANES = OWNED * BINS
DEPTH = 256
GRAD_ROWS = NODES * OUTPUTS
SUM_ROWS = GRAD_ROWS + NODES
WIRE_ROWS = GRAD_ROWS + 4 * NODES
STEPS = 8.0
TOP = 32000.0
HESS_UNIT = 512.0
HESS_SPLIT = 4096.0
ROW = ("xh", "zh", "zl", "c")
FEAT = ("y", "xl")
ALL = ROW + FEAT
NEAR = ("xh", "zl", "y", "xl")
f32 = jnp.float32
bf16 = jnp.bfloat16

ridge_term = 1.0


def pay_kernel(grad_hbm, hess_hbm, nodes_hbm, pay, grad, hess, nodes, sems):
    copies = [
        pltpu.make_async_copy(src, dst, sems.at[i])
        for i, (src, dst) in enumerate(
            ((grad_hbm, grad), (hess_hbm, hess), (nodes_hbm, nodes))
        )
    ]
    for copy in copies:
        copy.start()
    for copy in copies:
        copy.wait()
    column = lax.axis_index(FEAT)
    blocks = grad.shape[1] // 128
    node = nodes[0:blocks, :]
    for s in range(1, nodes.shape[0] // blocks):
        node = jnp.where(column == s, nodes[s * blocks : (s + 1) * blocks, :], node)
    rest = jnp.concatenate(
        [
            hess[...].astype(f32),
            node.astype(f32),
            jnp.zeros((pay.shape[1] - (OUTPUTS + 2) * blocks, 128), f32),
        ],
        axis=0,
    ).astype(bf16)
    grads = [grad[:, 128 * i : 128 * (i + 1)] for i in range(blocks)]
    for s in range(pay.shape[0]):
        for i in range(blocks):
            pay[s, OUTPUTS * i : OUTPUTS * (i + 1), :] = grads[i]
        pay[s, OUTPUTS * blocks :, :] = rest


def payload(gradient, hessian, row_node, near):
    blocks = gradient.shape[1] // 128
    pay_rows = OUTPUTS * blocks + -(-2 * blocks // 8) * 8
    hessian = hessian.reshape(blocks, 128)
    row_node = row_node.reshape(-1, 128)
    return pl.pallas_call(
        pay_kernel,
        out_shape=jax.ShapeDtypeStruct((near, pay_rows, 128), bf16),
        in_specs=[pl.BlockSpec(memory_space=pl.ANY)] * 3,
        scratch_shapes=[
            pltpu.VMEM(gradient.shape, bf16),
            pltpu.VMEM(hessian.shape, bf16),
            pltpu.VMEM(row_node.shape, jnp.int32),
            pltpu.SemaphoreType.DMA((3,)),
        ],
        name="payload",
    )(gradient, hessian, row_node)


def cut_kernel(bins_hbm, p0, p1, p2, p3, bins, sems):
    xh, zl, c = lax.axis_index("xh"), lax.axis_index("zl"), lax.axis_index("c")
    tile = 2 * OWNED
    part = bins.shape[0] // sems.shape[0]
    copies = [
        pltpu.make_async_copy(
            bins_hbm.at[i * part : (i + 1) * part], bins.at[i * part : (i + 1) * part], sems.at[i]
        )
        for i in range(sems.shape[0])
    ]
    for copy in copies:
        copy.start()
    for copy in copies:
        copy.wait()
    depth = p0.shape[1]
    for r, out in enumerate((p0, p1, p2, p3)):
        for j in range(depth):
            t = ((xh ^ (r // 2)) * depth + j) * 2 + (zl ^ (r % 2))
            both = bins[pl.ds(pl.multiple_of(t * tile, tile), tile), :].astype(f32)
            first, second = both[0:OWNED], both[OWNED:tile]
            out[0, j] = jnp.where(c == 0, first, second).astype(bf16)
            out[1, j] = jnp.where(c == 0, second, first).astype(bf16)


def cut_by_neighbour(bin_index):
    features, shard_rows = bin_index.shape
    shape = jax.ShapeDtypeStruct((2, features // (8 * OWNED), OWNED, shard_rows), bf16)
    return pl.pallas_call(
        cut_kernel,
        out_shape=(shape,) * 4,
        in_specs=[pl.BlockSpec(memory_space=pl.ANY)],
        scratch_shapes=[
            pltpu.VMEM(bin_index.shape, jnp.int32),
            pltpu.SemaphoreType.DMA((4,)),
        ],
        compiler_params=pltpu.CompilerParams(vmem_limit_bytes=32 << 20),
        name="cut_bins",
    )(bin_index)


def sums_kernel(places, pay, *refs):
    pieces, before, out = refs[: len(places)], refs[len(places) : -1], refs[-1]
    blocks = out.shape[0]
    columns = pay.shape[0] // 4
    layers = pay.shape[1] // OUTPUTS
    tiles = pieces[0].shape[-1] // DEPTH
    xh, zl = lax.axis_index("xh"), lax.axis_index("zl")

    def body(*sums):
        level = lax.broadcasted_iota(jnp.int32, (BINS, DEPTH), 0).astype(f32).astype(bf16)
        node_of_row = lax.broadcasted_iota(jnp.int32, (16, 128), 0).astype(f32).astype(bf16)
        one, zero = jnp.array(1, bf16), jnp.array(0, bf16)

        def by_node(group, layer):
            shard, i = group * columns + layer // layers, layer % layers
            grad = pay[shard, OUTPUTS * i : OUTPUTS * (i + 1), :]
            i = OUTPUTS * layers + i
            hess = jnp.broadcast_to(pay[shard, i : i + 1, :], (16, 128))
            i = i + layers
            node = jnp.broadcast_to(pay[shard, i : i + 1, :], (16, 128))
            rows = []
            for n in range(NODES):
                here = node == jnp.array(n, bf16)
                rows += [jnp.where(here, grad[k : k + 16], zero) for k in range(0, OUTPUTS, 16)]
            rows.append(jnp.where(node == node_of_row, hess, zero))
            return jnp.concatenate(rows, axis=0)

        def upto(bins):
            return jnp.concatenate(
                [
                    jnp.where(jnp.broadcast_to(bins[f : f + 1], (BINS, DEPTH)) <= level, one, zero)
                    for f in range(OWNED)
                ],
                axis=0,
            )

        for r, piece in zip(places, pieces):
            group = (xh ^ (r // 2)) * 2 + (zl ^ (r % 2))
            for t in range(tiles):
                values = jnp.concatenate(
                    [by_node(group, t * (DEPTH // 128) + k) for k in range(DEPTH // 128)], axis=1
                )
                for j in range(0, blocks, 2):
                    slot = j // 2 % 2
                    for m in range(2):
                        bins = piece[0, j + m, :, t * DEPTH : (t + 1) * DEPTH]
                        pltpu.matmul_push_rhs(upto(bins), slot, m, transpose=True)
                    for m in range(2):
                        pltpu.matmul_acc_lhs(sums[j + m], values, load_staged_rhs=slot)
        for j in range(blocks):
            total = pltpu.matmul_pop(sums[j])[0:SUM_ROWS]
            for term in before:
                total = total + term[j]
            out[j] = total

    pl.run_scoped(body, *[pltpu.ACC(j % 2)((GRAD_ROWS + 16, LANES), f32) for j in range(blocks)])


def local_sums(core, places, pay, pieces, before=()):
    halves, blocks, owned, shard_rows = pieces[0].shape
    bins_spec = pl.BlockSpec((1, blocks, owned, shard_rows), lambda j: (core, 0, 0, 0))
    pay_spec = pl.BlockSpec(pay.shape, lambda j: (0, 0, 0))
    flops = 2 * SUM_ROWS * len(places) * shard_rows * LANES * blocks
    return pl.pallas_call(
        functools.partial(sums_kernel, places),
        out_shape=jax.ShapeDtypeStruct((blocks, SUM_ROWS, LANES), f32),
        grid=(1,),
        in_specs=[pay_spec]
        + [bins_spec] * len(places)
        + [pl.BlockSpec((blocks, SUM_ROWS, LANES), lambda j: (0, 0, 0))] * len(before),
        out_specs=pl.BlockSpec((blocks, SUM_ROWS, LANES), lambda j: (0, 0, 0)),
        cost_estimate=pl.CostEstimate(flops=flops, bytes_accessed=1 << 21, transcendentals=0),
        compiler_params=pltpu.CompilerParams(vmem_limit_bytes=32 << 20),
        name="left_sums",
    )(pay, *pieces, *before)


def wire_kernel(mine, theirs, out):
    sums = mine[0] + theirs[0]
    grads = sums[0:GRAD_ROWS].reshape(NODES, OUTPUTS, LANES)
    largest = jnp.max(jnp.abs(grads), axis=1)
    octave = jnp.ceil(jnp.log2(jnp.maximum(largest, 1e-30)) * STEPS + 0.01)
    factor = TOP * jnp.exp2(octave * (-1.0 / STEPS))
    scaled = jnp.floor(grads * factor[:, None, :] + 0.5).reshape(GRAD_ROWS, LANES)
    out[0, 0:GRAD_ROWS, :] = scaled.astype(jnp.int32).astype(jnp.int16)
    units = sums[GRAD_ROWS:SUM_ROWS] * HESS_UNIT
    high = jnp.floor(units * (1.0 / HESS_SPLIT))
    low = units - high * HESS_SPLIT
    rest = jnp.concatenate([octave, high, low, jnp.zeros_like(low)], axis=0)
    out[0, GRAD_ROWS:WIRE_ROWS, :] = rest.astype(jnp.int32).astype(jnp.int16)


def to_wire(mine, theirs):
    blocks = mine.shape[0]
    sums_spec = pl.BlockSpec((1, SUM_ROWS, LANES), lambda j: (j, 0, 0))
    return pl.pallas_call(
        wire_kernel,
        out_shape=jax.ShapeDtypeStruct((blocks, WIRE_ROWS, LANES), jnp.int16),
        grid=(blocks,),
        in_specs=[sums_spec] * 2,
        out_specs=pl.BlockSpec((1, WIRE_ROWS, LANES), lambda j: (j, 0, 0)),
        compiler_params=pltpu.CompilerParams(vmem_limit_bytes=24 << 20),
        name="to_wire",
    )(mine, theirs)


def score_kernel(devices, parts, gain_out, best_out):
    left = jnp.zeros((NODES, OUTPUTS, LANES), f32)
    left_hess = jnp.zeros((NODES, LANES), f32)
    for s in range(parts.shape[0]):
        scaled = parts[s, 0:GRAD_ROWS, :].astype(jnp.int32).astype(f32)
        rest = parts[s, GRAD_ROWS:WIRE_ROWS, :].astype(jnp.int32).astype(f32)
        unit = jnp.exp2(rest[0:NODES] * (1.0 / STEPS)) * (1.0 / TOP)
        left = left + scaled.reshape(NODES, OUTPUTS, LANES) * unit[:, None, :]
        left_hess = left_hess + (
            rest[NODES : 2 * NODES] * HESS_SPLIT + rest[2 * NODES : 3 * NODES]
        ) * (1.0 / HESS_UNIT)
    whole = left[:, :, LANES - 1 :]
    whole_hess = left_hess[:, LANES - 1 :]
    right = whole - left
    right_hess = whole_hess - left_hess

    def part_score(sums, hess):
        return jnp.sum(sums * sums, axis=1) / (hess + ridge_term)

    terms = part_score(left, left_hess) + part_score(right, right_hess)
    gain = (0.5 / OUTPUTS) * (terms - part_score(whole, whole_hess))
    for f in range(OWNED):
        for n in range(NODES):
            gain_out[f : f + 1, n * BINS : (n + 1) * BINS] = gain[
                n : n + 1, f * BINS : (f + 1) * BINS
            ]
    best = jnp.max(gain, axis=1, keepdims=True)
    sublane = lax.broadcasted_iota(jnp.int32, (NODES, 128), 0)
    lane = lax.broadcasted_iota(jnp.int32, (NODES, 128), 1)
    turned = jnp.max(jnp.where(sublane == lane, best, -jnp.inf), axis=0, keepdims=True)
    best_out[...] = jnp.broadcast_to(turned[:, 0:NODES], (devices, NODES))


def final_scores(parts, devices):
    return pl.pallas_call(
        lambda *refs: score_kernel(devices, *refs),
        out_shape=(
            jax.ShapeDtypeStruct((OWNED, NODES * BINS), f32),
            jax.ShapeDtypeStruct((devices, NODES), f32),
        ),
        compiler_params=pltpu.CompilerParams(vmem_limit_bytes=48 << 20),
        name="split_scores",
    )(parts)


def on_device(bin_index, gradient, hessian, row_node):
    swap = [(0, 1), (1, 0)]
    pay = payload(gradient, hessian, row_node, lax.axis_size(NEAR))
    pay = lax.all_to_all(pay, NEAR, 0, 0, tiled=True)
    pieces = list(cut_by_neighbour(bin_index))
    pieces[1] = lax.ppermute(pieces[1], "zl", swap)
    pieces[2] = lax.ppermute(pieces[2], "xh", swap)
    pieces[3] = lax.ppermute(pieces[3], ("xh", "zl"), [(0, 3), (1, 2), (2, 1), (3, 0)])
    near = [local_sums(core, (0,), pay, pieces[:1]) for core in range(2)]
    near, pieces[1:] = lax.optimization_barrier((near, pieces[1:]))
    theirs = local_sums(1, (1, 2, 3), pay, pieces[1:], (near[1],))
    theirs = lax.ppermute(theirs, "c", swap)
    sums = to_wire(local_sums(0, (1, 2, 3), pay, pieces[1:], (near[0],)), theirs)
    parts = lax.all_to_all(sums, "zh", 0, 0, tiled=True)
    gain, best = final_scores(parts, lax.axis_size(ALL))
    best = lax.all_to_all(best, ALL, 0, 0, tiled=True)
    return gain, jnp.max(best, axis=0)


def solution(mesh):
    split = Mesh(mesh.devices.reshape(2, 4, 2, 2, 4, 2), ALL)
    in_specs = (P(FEAT, ROW), P(None, ROW + FEAT), P(ROW + FEAT), P(ROW))
    out_specs = (P(FEAT + ROW, None), P())
    return jax.shard_map(
        on_device, mesh=split, in_specs=in_specs, out_specs=out_specs, check_vma=False
    )
```

```python
import functools

import jax
import jax.numpy as jnp
from jax import lax
from jax.experimental import pallas as pl
from jax.experimental.pallas import tpu as pltpu
from jax.sharding import Mesh
from jax.sharding import PartitionSpec as P

BINS = 64
NODES = 8
OUTPUTS = 32
OWNED = 4
LANES = OWNED * BINS
DEPTH = 256
GRAD_ROWS = NODES * OUTPUTS
SUM_ROWS = GRAD_ROWS + NODES
WIRE_ROWS = GRAD_ROWS + 4 * NODES
STEPS = 8.0
TOP = 32000.0
HESS_UNIT = 512.0
HESS_SPLIT = 4096.0
ROW = ("xh", "zh", "zl", "c")
FEAT = ("y", "xl")
ALL = ROW + FEAT
NEAR = ("xh", "zl", "y", "xl")
f32 = jnp.float32
bf16 = jnp.bfloat16

ridge_term = 1.0


def pay_kernel(grad_hbm, hess_hbm, nodes_hbm, pay, grad, hess, nodes, sems):
    copies = [
        pltpu.make_async_copy(src, dst, sems.at[i])
        for i, (src, dst) in enumerate(
            ((grad_hbm, grad), (hess_hbm, hess), (nodes_hbm, nodes))
        )
    ]
    for copy in copies:
        copy.start()
    for copy in copies:
        copy.wait()
    column = lax.axis_index(FEAT)
    blocks = grad.shape[1] // 128
    node = nodes[0:blocks, :]
    for s in range(1, nodes.shape[0] // blocks):
        node = jnp.where(column == s, nodes[s * blocks : (s + 1) * blocks, :], node)
    rest = jnp.concatenate(
        [
            hess[...].astype(f32),
            node.astype(f32),
            jnp.zeros((pay.shape[1] - (OUTPUTS + 2) * blocks, 128), f32),
        ],
        axis=0,
    ).astype(bf16)
    grads = [grad[:, 128 * i : 128 * (i + 1)] for i in range(blocks)]
    for s in range(pay.shape[0]):
        for i in range(blocks):
            pay[s, OUTPUTS * i : OUTPUTS * (i + 1), :] = grads[i]
        pay[s, OUTPUTS * blocks :, :] = rest


def payload(gradient, hessian, row_node, near):
    blocks = gradient.shape[1] // 128
    pay_rows = OUTPUTS * blocks + -(-2 * blocks // 8) * 8
    hessian = hessian.reshape(blocks, 128)
    row_node = row_node.reshape(-1, 128)
    return pl.pallas_call(
        pay_kernel,
        out_shape=jax.ShapeDtypeStruct((near, pay_rows, 128), bf16),
        in_specs=[pl.BlockSpec(memory_space=pl.ANY)] * 3,
        scratch_shapes=[
            pltpu.VMEM(gradient.shape, bf16),
            pltpu.VMEM(hessian.shape, bf16),
            pltpu.VMEM(row_node.shape, jnp.int32),
            pltpu.SemaphoreType.DMA((3,)),
        ],
        name="payload",
    )(gradient, hessian, row_node)


def cut_kernel(bins_hbm, p0, p1, p2, p3, bins, sems):
    xh, zl, c = lax.axis_index("xh"), lax.axis_index("zl"), lax.axis_index("c")
    tile = 2 * OWNED
    part = bins.shape[0] // sems.shape[0]
    copies = [
        pltpu.make_async_copy(
            bins_hbm.at[i * part : (i + 1) * part], bins.at[i * part : (i + 1) * part], sems.at[i]
        )
        for i in range(sems.shape[0])
    ]
    for copy in copies:
        copy.start()
    for copy in copies:
        copy.wait()
    depth = p0.shape[1]
    for r, out in enumerate((p0, p1, p2, p3)):
        for j in range(depth):
            t = ((xh ^ (r // 2)) * depth + j) * 2 + (zl ^ (r % 2))
            both = bins[pl.ds(pl.multiple_of(t * tile, tile), tile), :].astype(f32)
            first, second = both[0:OWNED], both[OWNED:tile]
            out[0, j] = jnp.where(c == 0, first, second).astype(bf16)
            out[1, j] = jnp.where(c == 0, second, first).astype(bf16)


def cut_by_neighbour(bin_index):
    features, shard_rows = bin_index.shape
    shape = jax.ShapeDtypeStruct((2, features // (8 * OWNED), OWNED, shard_rows), bf16)
    return pl.pallas_call(
        cut_kernel,
        out_shape=(shape,) * 4,
        in_specs=[pl.BlockSpec(memory_space=pl.ANY)],
        scratch_shapes=[
            pltpu.VMEM(bin_index.shape, jnp.int32),
            pltpu.SemaphoreType.DMA((4,)),
        ],
        compiler_params=pltpu.CompilerParams(vmem_limit_bytes=32 << 20),
        name="cut_bins",
    )(bin_index)


def sums_kernel(places, pay, *refs):
    pieces, before, out = refs[: len(places)], refs[len(places) : -1], refs[-1]
    blocks = out.shape[0]
    columns = pay.shape[0] // 4
    layers = pay.shape[1] // OUTPUTS
    tiles = pieces[0].shape[-1] // DEPTH
    xh, zl = lax.axis_index("xh"), lax.axis_index("zl")

    def body(*sums):
        level = lax.broadcasted_iota(jnp.int32, (BINS, DEPTH), 0).astype(f32).astype(bf16)
        node_of_row = lax.broadcasted_iota(jnp.int32, (16, 128), 0).astype(f32).astype(bf16)
        one, zero = jnp.array(1, bf16), jnp.array(0, bf16)

        def by_node(group, layer):
            shard, i = group * columns + layer // layers, layer % layers
            grad = pay[shard, OUTPUTS * i : OUTPUTS * (i + 1), :]
            i = OUTPUTS * layers + i
            hess = jnp.broadcast_to(pay[shard, i : i + 1, :], (16, 128))
            i = i + layers
            node = jnp.broadcast_to(pay[shard, i : i + 1, :], (16, 128))
            rows = []
            for n in range(NODES):
                here = node == jnp.array(n, bf16)
                rows += [jnp.where(here, grad[k : k + 16], zero) for k in range(0, OUTPUTS, 16)]
            rows.append(jnp.where(node == node_of_row, hess, zero))
            return jnp.concatenate(rows, axis=0)

        def upto(bins):
            return jnp.concatenate(
                [
                    jnp.where(jnp.broadcast_to(bins[f : f + 1], (BINS, DEPTH)) <= level, one, zero)
                    for f in range(OWNED)
                ],
                axis=0,
            )

        for r, piece in zip(places, pieces):
            group = (xh ^ (r // 2)) * 2 + (zl ^ (r % 2))
            for t in range(tiles):
                values = jnp.concatenate(
                    [by_node(group, t * (DEPTH // 128) + k) for k in range(DEPTH // 128)], axis=1
                )
                for j in range(0, blocks, 2):
                    slot = j // 2 % 2
                    for m in range(2):
                        bins = piece[0, j + m, :, t * DEPTH : (t + 1) * DEPTH]
                        pltpu.matmul_push_rhs(upto(bins), slot, m, transpose=True)
                    for m in range(2):
                        pltpu.matmul_acc_lhs(sums[j + m], values, load_staged_rhs=slot)
        for j in range(blocks):
            total = pltpu.matmul_pop(sums[j])[0:SUM_ROWS]
            for term in before:
                total = total + term[j]
            out[j] = total

    pl.run_scoped(body, *[pltpu.ACC(j % 2)((GRAD_ROWS + 16, LANES), f32) for j in range(blocks)])


def local_sums(core, places, pay, pieces, before=()):
    halves, blocks, owned, shard_rows = pieces[0].shape
    bins_spec = pl.BlockSpec((1, blocks, owned, shard_rows), lambda j: (core, 0, 0, 0))
    pay_spec = pl.BlockSpec(pay.shape, lambda j: (0, 0, 0))
    flops = 2 * SUM_ROWS * len(places) * shard_rows * LANES * blocks
    return pl.pallas_call(
        functools.partial(sums_kernel, places),
        out_shape=jax.ShapeDtypeStruct((blocks, SUM_ROWS, LANES), f32),
        grid=(1,),
        in_specs=[pay_spec]
        + [bins_spec] * len(places)
        + [pl.BlockSpec((blocks, SUM_ROWS, LANES), lambda j: (0, 0, 0))] * len(before),
        out_specs=pl.BlockSpec((blocks, SUM_ROWS, LANES), lambda j: (0, 0, 0)),
        cost_estimate=pl.CostEstimate(flops=flops, bytes_accessed=1 << 21, transcendentals=0),
        compiler_params=pltpu.CompilerParams(vmem_limit_bytes=32 << 20),
        name="left_sums",
    )(pay, *pieces, *before)


def wire_kernel(mine, theirs, out):
    sums = mine[0] + theirs[0]
    grads = sums[0:GRAD_ROWS].reshape(NODES, OUTPUTS, LANES)
    largest = jnp.max(jnp.abs(grads), axis=1)
    octave = jnp.ceil(jnp.log2(jnp.maximum(largest, 1e-30)) * STEPS + 0.01)
    factor = TOP * jnp.exp2(octave * (-1.0 / STEPS))
    scaled = jnp.floor(grads * factor[:, None, :] + 0.5).reshape(GRAD_ROWS, LANES)
    out[0, 0:GRAD_ROWS, :] = scaled.astype(jnp.int32).astype(jnp.int16)
    units = sums[GRAD_ROWS:SUM_ROWS] * HESS_UNIT
    high = jnp.floor(units * (1.0 / HESS_SPLIT))
    low = units - high * HESS_SPLIT
    rest = jnp.concatenate([octave, high, low, jnp.zeros_like(low)], axis=0)
    out[0, GRAD_ROWS:WIRE_ROWS, :] = rest.astype(jnp.int32).astype(jnp.int16)


def to_wire(mine, theirs):
    blocks = mine.shape[0]
    sums_spec = pl.BlockSpec((1, SUM_ROWS, LANES), lambda j: (j, 0, 0))
    return pl.pallas_call(
        wire_kernel,
        out_shape=jax.ShapeDtypeStruct((blocks, WIRE_ROWS, LANES), jnp.int16),
        grid=(blocks,),
        in_specs=[sums_spec] * 2,
        out_specs=pl.BlockSpec((1, WIRE_ROWS, LANES), lambda j: (j, 0, 0)),
        compiler_params=pltpu.CompilerParams(vmem_limit_bytes=24 << 20),
        name="to_wire",
    )(mine, theirs)


def score_kernel(devices, parts, gain_out, best_out):
    left = jnp.zeros((NODES, OUTPUTS, LANES), f32)
    left_hess = jnp.zeros((NODES, LANES), f32)
    for s in range(parts.shape[0]):
        scaled = parts[s, 0:GRAD_ROWS, :].astype(jnp.int32).astype(f32)
        rest = parts[s, GRAD_ROWS:WIRE_ROWS, :].astype(jnp.int32).astype(f32)
        unit = jnp.exp2(rest[0:NODES] * (1.0 / STEPS)) * (1.0 / TOP)
        left = left + scaled.reshape(NODES, OUTPUTS, LANES) * unit[:, None, :]
        left_hess = left_hess + (
            rest[NODES : 2 * NODES] * HESS_SPLIT + rest[2 * NODES : 3 * NODES]
        ) * (1.0 / HESS_UNIT)
    whole = left[:, :, LANES - 1 :]
    whole_hess = left_hess[:, LANES - 1 :]
    right = whole - left
    right_hess = whole_hess - left_hess

    def part_score(sums, hess):
        return jnp.sum(sums * sums, axis=1) / (hess + ridge_term)

    terms = part_score(left, left_hess) + part_score(right, right_hess)
    gain = (0.5 / OUTPUTS) * (terms - part_score(whole, whole_hess))
    for f in range(OWNED):
        for n in range(NODES):
            gain_out[f : f + 1, n * BINS : (n + 1) * BINS] = gain[
                n : n + 1, f * BINS : (f + 1) * BINS
            ]
    best = jnp.max(gain, axis=1, keepdims=True)
    sublane = lax.broadcasted_iota(jnp.int32, (NODES, 128), 0)
    lane = lax.broadcasted_iota(jnp.int32, (NODES, 128), 1)
    turned = jnp.max(jnp.where(sublane == lane, best, -jnp.inf), axis=0, keepdims=True)
    best_out[...] = jnp.broadcast_to(turned[:, 0:NODES], (devices, NODES))


def final_scores(parts, devices):
    return pl.pallas_call(
        lambda *refs: score_kernel(devices, *refs),
        out_shape=(
            jax.ShapeDtypeStruct((OWNED, NODES * BINS), f32),
            jax.ShapeDtypeStruct((devices, NODES), f32),
        ),
        compiler_params=pltpu.CompilerParams(vmem_limit_bytes=48 << 20),
        name="split_scores",
    )(parts)


def on_device(bin_index, gradient, hessian, row_node):
    swap = [(0, 1), (1, 0)]
    pay = payload(gradient, hessian, row_node, lax.axis_size(NEAR))
    pay = lax.all_to_all(pay, NEAR, 0, 0, tiled=True)
    pieces = list(cut_by_neighbour(bin_index))
    pieces[1] = lax.ppermute(pieces[1], "zl", swap)
    pieces[2] = lax.ppermute(pieces[2], "xh", swap)
    pieces[3] = lax.ppermute(pieces[3], ("xh", "zl"), [(0, 3), (1, 2), (2, 1), (3, 0)])
    near = [None, local_sums(1, (0,), pay, pieces[:1])]
    near[1], pieces[1] = lax.optimization_barrier((near[1], pieces[1]))
    near[0] = local_sums(0, (0, 1), pay, pieces[:2])
    near, pieces[2:] = lax.optimization_barrier((near, pieces[2:]))
    theirs = local_sums(1, (1, 2, 3), pay, pieces[1:], (near[1],))
    theirs = lax.ppermute(theirs, "c", swap)
    sums = to_wire(local_sums(0, (2, 3), pay, pieces[2:], (near[0],)), theirs)
    parts = lax.all_to_all(sums, "zh", 0, 0, tiled=True)
    gain, best = final_scores(parts, lax.axis_size(ALL))
    best = lax.all_to_all(best, ALL, 0, 0, tiled=True)
    return gain, jnp.max(best, axis=0)


def solution(mesh):
    split = Mesh(mesh.devices.reshape(2, 4, 2, 2, 4, 2), ALL)
    in_specs = (P(FEAT, ROW), P(None, ROW + FEAT), P(ROW + FEAT), P(ROW))
    out_specs = (P(FEAT + ROW, None), P())
    return jax.shard_map(
        on_device, mesh=split, in_specs=in_specs, out_specs=out_specs, check_vma=False
    )
```

```python
import functools

import jax
import jax.numpy as jnp
from jax import lax
from jax.experimental import pallas as pl
from jax.experimental.pallas import tpu as pltpu
from jax.sharding import Mesh
from jax.sharding import PartitionSpec as P

BINS = 64
NODES = 8
OUTPUTS = 32
OWNED = 4
LANES = OWNED * BINS
DEPTH = 256
GRAD_ROWS = NODES * OUTPUTS
SUM_ROWS = GRAD_ROWS + NODES
WIRE_ROWS = GRAD_ROWS + 4 * NODES
STEPS = 8.0
TOP = 32000.0
HESS_UNIT = 512.0
HESS_SPLIT = 4096.0
ROW = ("xh", "zh", "zl", "c")
FEAT = ("y", "xl")
ALL = ROW + FEAT
NEAR = ("xh", "zl", "y", "xl")
f32 = jnp.float32
bf16 = jnp.bfloat16

ridge_term = 1.0


def pay_kernel(grad_hbm, hess_hbm, nodes_hbm, pay, grad, hess, nodes, sems):
    copies = [
        pltpu.make_async_copy(src, dst, sems.at[i])
        for i, (src, dst) in enumerate(
            ((grad_hbm, grad), (hess_hbm, hess), (nodes_hbm, nodes))
        )
    ]
    for copy in copies:
        copy.start()
    for copy in copies:
        copy.wait()
    column = lax.axis_index(FEAT)
    blocks = grad.shape[1] // 128
    node = nodes[0:blocks, :]
    for s in range(1, nodes.shape[0] // blocks):
        node = jnp.where(column == s, nodes[s * blocks : (s + 1) * blocks, :], node)
    rest = jnp.concatenate(
        [
            hess[...].astype(f32),
            node.astype(f32),
            jnp.zeros((pay.shape[1] - (OUTPUTS + 2) * blocks, 128), f32),
        ],
        axis=0,
    ).astype(bf16)
    grads = [grad[:, 128 * i : 128 * (i + 1)] for i in range(blocks)]
    for s in range(pay.shape[0]):
        for i in range(blocks):
            pay[s, OUTPUTS * i : OUTPUTS * (i + 1), :] = grads[i]
        pay[s, OUTPUTS * blocks :, :] = rest


def payload(gradient, hessian, row_node, near):
    blocks = gradient.shape[1] // 128
    pay_rows = OUTPUTS * blocks + -(-2 * blocks // 8) * 8
    hessian = hessian.reshape(blocks, 128)
    row_node = row_node.reshape(-1, 128)
    return pl.pallas_call(
        pay_kernel,
        out_shape=jax.ShapeDtypeStruct((near, pay_rows, 128), bf16),
        in_specs=[pl.BlockSpec(memory_space=pl.ANY)] * 3,
        scratch_shapes=[
            pltpu.VMEM(gradient.shape, bf16),
            pltpu.VMEM(hessian.shape, bf16),
            pltpu.VMEM(row_node.shape, jnp.int32),
            pltpu.SemaphoreType.DMA((3,)),
        ],
        name="payload",
    )(gradient, hessian, row_node)


def cut_kernel(bins_hbm, p0, p1, p2, p3, bins, sems):
    xh, zl, c = lax.axis_index("xh"), lax.axis_index("zl"), lax.axis_index("c")
    tile = 2 * OWNED
    part = bins.shape[0] // sems.shape[0]
    copies = [
        pltpu.make_async_copy(
            bins_hbm.at[i * part : (i + 1) * part], bins.at[i * part : (i + 1) * part], sems.at[i]
        )
        for i in range(sems.shape[0])
    ]
    for copy in copies:
        copy.start()
    for copy in copies:
        copy.wait()
    depth = p0.shape[1]
    for r, out in enumerate((p0, p1, p2, p3)):
        for j in range(depth):
            t = ((xh ^ (r // 2)) * depth + j) * 2 + (zl ^ (r % 2))
            both = bins[pl.ds(pl.multiple_of(t * tile, tile), tile), :].astype(f32)
            first, second = both[0:OWNED], both[OWNED:tile]
            out[0, j] = jnp.where(c == 0, first, second).astype(bf16)
            out[1, j] = jnp.where(c == 0, second, first).astype(bf16)


def cut_by_neighbour(bin_index):
    features, shard_rows = bin_index.shape
    shape = jax.ShapeDtypeStruct((2, features // (8 * OWNED), OWNED, shard_rows), bf16)
    return pl.pallas_call(
        cut_kernel,
        out_shape=(shape,) * 4,
        in_specs=[pl.BlockSpec(memory_space=pl.ANY)],
        scratch_shapes=[
            pltpu.VMEM(bin_index.shape, jnp.int32),
            pltpu.SemaphoreType.DMA((4,)),
        ],
        compiler_params=pltpu.CompilerParams(vmem_limit_bytes=32 << 20),
        name="cut_bins",
    )(bin_index)


def sums_kernel(places, pay, *refs):
    pieces, before, out = refs[: len(places)], refs[len(places) : -1], refs[-1]
    blocks = out.shape[0]
    columns = pay.shape[0] // 4
    layers = pay.shape[1] // OUTPUTS
    tiles = pieces[0].shape[-1] // DEPTH
    xh, zl = lax.axis_index("xh"), lax.axis_index("zl")

    def body(*sums):
        level = lax.broadcasted_iota(jnp.int32, (BINS, DEPTH), 0).astype(f32).astype(bf16)
        node_of_row = lax.broadcasted_iota(jnp.int32, (16, 128), 0).astype(f32).astype(bf16)
        one, zero = jnp.array(1, bf16), jnp.array(0, bf16)

        def by_node(group, layer):
            shard, i = group * columns + layer // layers, layer % layers
            grad = pay[shard, OUTPUTS * i : OUTPUTS * (i + 1), :]
            i = OUTPUTS * layers + i
            hess = jnp.broadcast_to(pay[shard, i : i + 1, :], (16, 128))
            i = i + layers
            node = jnp.broadcast_to(pay[shard, i : i + 1, :], (16, 128))
            rows = []
            for n in range(NODES):
                here = node == jnp.array(n, bf16)
                rows += [jnp.where(here, grad[k : k + 16], zero) for k in range(0, OUTPUTS, 16)]
            rows.append(jnp.where(node == node_of_row, hess, zero))
            return jnp.concatenate(rows, axis=0)

        def upto(bins):
            return jnp.concatenate(
                [
                    jnp.where(jnp.broadcast_to(bins[f : f + 1], (BINS, DEPTH)) <= level, one, zero)
                    for f in range(OWNED)
                ],
                axis=0,
            )

        for r, piece in zip(places, pieces):
            group = (xh ^ (r // 2)) * 2 + (zl ^ (r % 2))
            for t in range(tiles):
                values = jnp.concatenate(
                    [by_node(group, t * (DEPTH // 128) + k) for k in range(DEPTH // 128)], axis=1
                )
                for j in range(0, blocks, 2):
                    slot = j // 2 % 2
                    for m in range(2):
                        bins = piece[0, j + m, :, t * DEPTH : (t + 1) * DEPTH]
                        pltpu.matmul_push_rhs(upto(bins), slot, m, transpose=True)
                    for m in range(2):
                        pltpu.matmul_acc_lhs(sums[j + m], values, load_staged_rhs=slot)
        for j in range(blocks):
            total = pltpu.matmul_pop(sums[j])[0:SUM_ROWS]
            for term in before:
                total = total + term[j]
            out[j] = total

    pl.run_scoped(body, *[pltpu.ACC(j % 2)((GRAD_ROWS + 16, LANES), f32) for j in range(blocks)])


def local_sums(core, places, pay, pieces, before=()):
    halves, blocks, owned, shard_rows = pieces[0].shape
    bins_spec = pl.BlockSpec((1, blocks, owned, shard_rows), lambda j: (core, 0, 0, 0))
    pay_spec = pl.BlockSpec(pay.shape, lambda j: (0, 0, 0))
    flops = 2 * SUM_ROWS * len(places) * shard_rows * LANES * blocks
    return pl.pallas_call(
        functools.partial(sums_kernel, places),
        out_shape=jax.ShapeDtypeStruct((blocks, SUM_ROWS, LANES), f32),
        grid=(1,),
        in_specs=[pay_spec]
        + [bins_spec] * len(places)
        + [pl.BlockSpec((blocks, SUM_ROWS, LANES), lambda j: (0, 0, 0))] * len(before),
        out_specs=pl.BlockSpec((blocks, SUM_ROWS, LANES), lambda j: (0, 0, 0)),
        cost_estimate=pl.CostEstimate(flops=flops, bytes_accessed=1 << 21, transcendentals=0),
        compiler_params=pltpu.CompilerParams(vmem_limit_bytes=32 << 20),
        name="left_sums",
    )(pay, *pieces, *before)


def wire_kernel(order, mine, theirs, *outs):
    zh, depth = lax.axis_index("zh"), mine.shape[0]
    for d, out in zip(order, outs):
        keeper = (zh + d) % depth
        sums = mine[keeper] + theirs[keeper]
        grads = sums[0:GRAD_ROWS].reshape(NODES, OUTPUTS, LANES)
        largest = jnp.max(jnp.abs(grads), axis=1)
        octave = jnp.ceil(jnp.log2(jnp.maximum(largest, 1e-30)) * STEPS + 0.01)
        factor = TOP * jnp.exp2(octave * (-1.0 / STEPS))
        scaled = jnp.floor(grads * factor[:, None, :] + 0.5).reshape(GRAD_ROWS, LANES)
        out[0:GRAD_ROWS, :] = scaled.astype(jnp.int32).astype(jnp.int16)
        units = sums[GRAD_ROWS:SUM_ROWS] * HESS_UNIT
        high = jnp.floor(units * (1.0 / HESS_SPLIT))
        low = units - high * HESS_SPLIT
        rest = jnp.concatenate([octave, high, low, jnp.zeros_like(low)], axis=0)
        out[GRAD_ROWS:WIRE_ROWS, :] = rest.astype(jnp.int32).astype(jnp.int16)


def to_wire(order, mine, theirs):
    return pl.pallas_call(
        functools.partial(wire_kernel, order),
        out_shape=(jax.ShapeDtypeStruct((WIRE_ROWS, LANES), jnp.int16),) * len(order),
        compiler_params=pltpu.CompilerParams(vmem_limit_bytes=24 << 20),
        name="to_wire",
    )(mine, theirs)


def score_kernel(devices, *refs):
    parts, (gain_out, best_out) = refs[:-2], refs[-2:]
    left = jnp.zeros((NODES, OUTPUTS, LANES), f32)
    left_hess = jnp.zeros((NODES, LANES), f32)
    for part in parts:
        scaled = part[0:GRAD_ROWS, :].astype(jnp.int32).astype(f32)
        rest = part[GRAD_ROWS:WIRE_ROWS, :].astype(jnp.int32).astype(f32)
        unit = jnp.exp2(rest[0:NODES] * (1.0 / STEPS)) * (1.0 / TOP)
        left = left + scaled.reshape(NODES, OUTPUTS, LANES) * unit[:, None, :]
        left_hess = left_hess + (
            rest[NODES : 2 * NODES] * HESS_SPLIT + rest[2 * NODES : 3 * NODES]
        ) * (1.0 / HESS_UNIT)
    whole = left[:, :, LANES - 1 :]
    whole_hess = left_hess[:, LANES - 1 :]
    right = whole - left
    right_hess = whole_hess - left_hess

    def part_score(sums, hess):
        return jnp.sum(sums * sums, axis=1) / (hess + ridge_term)

    terms = part_score(left, left_hess) + part_score(right, right_hess)
    gain = (0.5 / OUTPUTS) * (terms - part_score(whole, whole_hess))
    for f in range(OWNED):
        for n in range(NODES):
            gain_out[f : f + 1, n * BINS : (n + 1) * BINS] = gain[
                n : n + 1, f * BINS : (f + 1) * BINS
            ]
    best = jnp.max(gain, axis=1, keepdims=True)
    sublane = lax.broadcasted_iota(jnp.int32, (NODES, 128), 0)
    lane = lax.broadcasted_iota(jnp.int32, (NODES, 128), 1)
    turned = jnp.max(jnp.where(sublane == lane, best, -jnp.inf), axis=0, keepdims=True)
    best_out[...] = jnp.broadcast_to(turned[:, 0:NODES], (devices, NODES))


def final_scores(parts, devices):
    return pl.pallas_call(
        functools.partial(score_kernel, devices),
        out_shape=(
            jax.ShapeDtypeStruct((OWNED, NODES * BINS), f32),
            jax.ShapeDtypeStruct((devices, NODES), f32),
        ),
        compiler_params=pltpu.CompilerParams(vmem_limit_bytes=48 << 20),
        name="split_scores",
    )(*parts)


def on_device(bin_index, gradient, hessian, row_node):
    swap = [(0, 1), (1, 0)]
    pay = payload(gradient, hessian, row_node, lax.axis_size(NEAR))
    pay = lax.all_to_all(pay, NEAR, 0, 0, tiled=True)
    pieces = list(cut_by_neighbour(bin_index))
    pieces[1] = lax.ppermute(pieces[1], "zl", swap)
    pieces[2] = lax.ppermute(pieces[2], "xh", swap)
    pieces[3] = lax.ppermute(pieces[3], ("xh", "zl"), [(0, 3), (1, 2), (2, 1), (3, 0)])
    near = [None, local_sums(1, (0,), pay, pieces[:1])]
    near[1], pieces[1] = lax.optimization_barrier((near[1], pieces[1]))
    near[0] = local_sums(0, (0, 1), pay, pieces[:2])
    near, pieces[2:] = lax.optimization_barrier((near, pieces[2:]))
    theirs = local_sums(1, (1, 2, 3), pay, pieces[1:], (near[1],))
    theirs = lax.ppermute(theirs, "c", swap)
    mine = local_sums(0, (2, 3), pay, pieces[2:], (near[0],))
    depth = lax.axis_size("zh")
    order = (2, 1, 3, 0)
    parts = [
        lax.ppermute(part, "zh", [(i, (i + d) % depth) for i in range(depth)]) if d else part
        for d, part in zip(order, to_wire(order, mine, theirs))
    ]
    gain, best = final_scores(parts, lax.axis_size(ALL))
    best = lax.all_to_all(best, ALL, 0, 0, tiled=True)
    return gain, jnp.max(best, axis=0)


def solution(mesh):
    split = Mesh(mesh.devices.reshape(2, 4, 2, 2, 4, 2), ALL)
    in_specs = (P(FEAT, ROW), P(None, ROW + FEAT), P(ROW + FEAT), P(ROW))
    out_specs = (P(FEAT + ROW, None), P())
    return jax.shard_map(
        on_device, mesh=split, in_specs=in_specs, out_specs=out_specs, check_vma=False
    )
```

```python
import functools

import jax
import jax.numpy as jnp
from jax import lax
from jax.experimental import pallas as pl
from jax.experimental.pallas import tpu as pltpu
from jax.sharding import Mesh
from jax.sharding import PartitionSpec as P

BINS = 64
NODES = 8
OUTPUTS = 32
OWNED = 4
LANES = OWNED * BINS
DEPTH = 256
GRAD_ROWS = NODES * OUTPUTS
SUM_ROWS = GRAD_ROWS + NODES
WIRE_ROWS = GRAD_ROWS + 4 * NODES
STEPS = 8.0
TOP = 32000.0
HESS_UNIT = 512.0
HESS_SPLIT = 4096.0
ROW = ("xh", "zh", "zl", "c")
FEAT = ("y", "xl")
ALL = ROW + FEAT
NEAR = ("xh", "zl", "y", "xl")
f32 = jnp.float32
bf16 = jnp.bfloat16

ridge_term = 1.0


def pay_kernel(grad_hbm, hess_hbm, nodes_hbm, pay, grad, hess, nodes, sems):
    copies = [
        pltpu.make_async_copy(src, dst, sems.at[i])
        for i, (src, dst) in enumerate(
            ((grad_hbm, grad), (hess_hbm, hess), (nodes_hbm, nodes))
        )
    ]
    for copy in copies:
        copy.start()
    for copy in copies:
        copy.wait()
    column = lax.axis_index(FEAT)
    blocks = grad.shape[1] // 128
    node = nodes[0:blocks, :]
    for s in range(1, nodes.shape[0] // blocks):
        node = jnp.where(column == s, nodes[s * blocks : (s + 1) * blocks, :], node)
    rest = jnp.concatenate(
        [
            hess[...].astype(f32),
            node.astype(f32),
            jnp.zeros((pay.shape[1] - (OUTPUTS + 2) * blocks, 128), f32),
        ],
        axis=0,
    ).astype(bf16)
    grads = [grad[:, 128 * i : 128 * (i + 1)] for i in range(blocks)]
    for s in range(pay.shape[0]):
        for i in range(blocks):
            pay[s, OUTPUTS * i : OUTPUTS * (i + 1), :] = grads[i]
        pay[s, OUTPUTS * blocks :, :] = rest


def payload(gradient, hessian, row_node, near):
    blocks = gradient.shape[1] // 128
    pay_rows = OUTPUTS * blocks + -(-2 * blocks // 8) * 8
    hessian = hessian.reshape(blocks, 128)
    row_node = row_node.reshape(-1, 128)
    return pl.pallas_call(
        pay_kernel,
        out_shape=jax.ShapeDtypeStruct((near, pay_rows, 128), bf16),
        in_specs=[pl.BlockSpec(memory_space=pl.ANY)] * 3,
        scratch_shapes=[
            pltpu.VMEM(gradient.shape, bf16),
            pltpu.VMEM(hessian.shape, bf16),
            pltpu.VMEM(row_node.shape, jnp.int32),
            pltpu.SemaphoreType.DMA((3,)),
        ],
        name="payload",
    )(gradient, hessian, row_node)


def cut_kernel(bins_hbm, p0, p1, p2, p3, bins, sems):
    xh, zl, c = lax.axis_index("xh"), lax.axis_index("zl"), lax.axis_index("c")
    tile = 2 * OWNED
    part = bins.shape[0] // sems.shape[0]
    copies = [
        pltpu.make_async_copy(
            bins_hbm.at[i * part : (i + 1) * part], bins.at[i * part : (i + 1) * part], sems.at[i]
        )
        for i in range(sems.shape[0])
    ]
    for copy in copies:
        copy.start()
    for copy in copies:
        copy.wait()
    depth = p0.shape[1]
    for r, out in enumerate((p0, p1, p2, p3)):
        for j in range(depth):
            t = ((xh ^ (r // 2)) * depth + j) * 2 + (zl ^ (r % 2))
            both = bins[pl.ds(pl.multiple_of(t * tile, tile), tile), :].astype(f32)
            first, second = both[0:OWNED], both[OWNED:tile]
            out[0, j] = jnp.where(c == 0, first, second).astype(bf16)
            out[1, j] = jnp.where(c == 0, second, first).astype(bf16)


def cut_by_neighbour(bin_index):
    features, shard_rows = bin_index.shape
    shape = jax.ShapeDtypeStruct((2, features // (8 * OWNED), OWNED, shard_rows), bf16)
    return pl.pallas_call(
        cut_kernel,
        out_shape=(shape,) * 4,
        in_specs=[pl.BlockSpec(memory_space=pl.ANY)],
        scratch_shapes=[
            pltpu.VMEM(bin_index.shape, jnp.int32),
            pltpu.SemaphoreType.DMA((4,)),
        ],
        compiler_params=pltpu.CompilerParams(vmem_limit_bytes=32 << 20),
        name="cut_bins",
    )(bin_index)


def sums_kernel(places, order, pay, *refs):
    pieces, before, out = refs[: len(places)], refs[len(places) : -1], refs[-1]
    pairs = len(order) // 2
    zh, depth = lax.axis_index("zh"), pieces[0].shape[1]
    columns = pay.shape[0] // 4
    layers = pay.shape[1] // OUTPUTS
    tiles = pieces[0].shape[-1] // DEPTH
    xh, zl = lax.axis_index("xh"), lax.axis_index("zl")

    def body(*sums):
        level = lax.broadcasted_iota(jnp.int32, (BINS, DEPTH), 0).astype(f32).astype(bf16)
        node_of_row = lax.broadcasted_iota(jnp.int32, (16, 128), 0).astype(f32).astype(bf16)
        one, zero = jnp.array(1, bf16), jnp.array(0, bf16)

        def by_node(group, layer):
            shard, i = group * columns + layer // layers, layer % layers
            grad = pay[shard, OUTPUTS * i : OUTPUTS * (i + 1), :]
            i = OUTPUTS * layers + i
            hess = jnp.broadcast_to(pay[shard, i : i + 1, :], (16, 128))
            i = i + layers
            node = jnp.broadcast_to(pay[shard, i : i + 1, :], (16, 128))
            rows = []
            for n in range(NODES):
                here = node == jnp.array(n, bf16)
                rows += [jnp.where(here, grad[k : k + 16], zero) for k in range(0, OUTPUTS, 16)]
            rows.append(jnp.where(node == node_of_row, hess, zero))
            return jnp.concatenate(rows, axis=0)

        def upto(bins):
            return jnp.concatenate(
                [
                    jnp.where(jnp.broadcast_to(bins[f : f + 1], (BINS, DEPTH)) <= level, one, zero)
                    for f in range(OWNED)
                ],
                axis=0,
            )

        for r, piece in zip(places, pieces):
            group = (xh ^ (r // 2)) * 2 + (zl ^ (r % 2))
            for t in range(tiles):
                values = jnp.concatenate(
                    [by_node(group, t * (DEPTH // 128) + k) for k in range(DEPTH // 128)], axis=1
                )
                def push(block, slot, m, piece=piece, t=t):
                    bins = piece[0, (zh + order[block]) % depth, :, t * DEPTH : (t + 1) * DEPTH]
                    pltpu.matmul_push_rhs(upto(bins), slot, m, transpose=True)

                for pair in range(pairs):
                    for m in range(2):
                        push(2 * pair + m, pair % 2, m)
                    for m in range(2):
                        pltpu.matmul_acc_lhs(sums[2 * pair + m], values, load_staged_rhs=pair % 2)
                if len(order) % 2:
                    slot = 1 if pairs else t // 2 % 2
                    push(2 * pairs, slot, t % 2)
                    pltpu.matmul_acc_lhs(sums[2 * pairs + t % 2], values, load_staged_rhs=slot)
        totals = [pltpu.matmul_pop(ref)[0:SUM_ROWS] for ref in sums]
        if len(order) % 2:
            totals[-2:] = [totals[-2] + totals[-1]]
        for j, total in enumerate(totals):
            for term in before:
                total = total + term[j]
            out[j] = total

    count = len(order) + len(order) % 2
    pl.run_scoped(body, *[pltpu.ACC(j % 2)((GRAD_ROWS + 16, LANES), f32) for j in range(count)])


def local_sums(core, places, order, pay, pieces, before=()):
    halves, depth, owned, shard_rows = pieces[0].shape
    blocks = len(order)
    bins_spec = pl.BlockSpec((1, depth, owned, shard_rows), lambda j: (core, 0, 0, 0))
    pay_spec = pl.BlockSpec(pay.shape, lambda j: (0, 0, 0))
    flops = 2 * SUM_ROWS * len(places) * shard_rows * LANES * blocks
    return pl.pallas_call(
        functools.partial(sums_kernel, places, order),
        out_shape=jax.ShapeDtypeStruct((blocks, SUM_ROWS, LANES), f32),
        grid=(1,),
        in_specs=[pay_spec]
        + [bins_spec] * len(places)
        + [pl.BlockSpec((blocks, SUM_ROWS, LANES), lambda j: (0, 0, 0))] * len(before),
        out_specs=pl.BlockSpec((blocks, SUM_ROWS, LANES), lambda j: (0, 0, 0)),
        cost_estimate=pl.CostEstimate(flops=flops, bytes_accessed=1 << 21, transcendentals=0),
        compiler_params=pltpu.CompilerParams(vmem_limit_bytes=32 << 20),
        name="left_sums",
    )(pay, *pieces, *before)


def wire_kernel(mine, theirs, *outs):
    for j, out in enumerate(outs):
        sums = mine[j] + theirs[j]
        grads = sums[0:GRAD_ROWS].reshape(NODES, OUTPUTS, LANES)
        largest = jnp.max(jnp.abs(grads), axis=1)
        octave = jnp.ceil(jnp.log2(jnp.maximum(largest, 1e-30)) * STEPS + 0.01)
        factor = TOP * jnp.exp2(octave * (-1.0 / STEPS))
        scaled = jnp.floor(grads * factor[:, None, :] + 0.5).reshape(GRAD_ROWS, LANES)
        out[0:GRAD_ROWS, :] = scaled.astype(jnp.int32).astype(jnp.int16)
        units = sums[GRAD_ROWS:SUM_ROWS] * HESS_UNIT
        high = jnp.floor(units * (1.0 / HESS_SPLIT))
        low = units - high * HESS_SPLIT
        rest = jnp.concatenate([octave, high, low, jnp.zeros_like(low)], axis=0)
        out[GRAD_ROWS:WIRE_ROWS, :] = rest.astype(jnp.int32).astype(jnp.int16)


def to_wire(mine, theirs):
    return pl.pallas_call(
        wire_kernel,
        out_shape=(jax.ShapeDtypeStruct((WIRE_ROWS, LANES), jnp.int16),) * mine.shape[0],
        compiler_params=pltpu.CompilerParams(vmem_limit_bytes=24 << 20),
        name="to_wire",
    )(mine, theirs)


def score_kernel(devices, *refs):
    (mine, theirs), parts, (gain_out, best_out) = refs[:2], refs[2:-2], refs[-2:]
    kept = mine[0] + theirs[theirs.shape[0] - 1]
    left = kept[0:GRAD_ROWS].reshape(NODES, OUTPUTS, LANES)
    left_hess = kept[GRAD_ROWS:SUM_ROWS]
    for part in parts:
        scaled = part[0:GRAD_ROWS, :].astype(jnp.int32).astype(f32)
        rest = part[GRAD_ROWS:WIRE_ROWS, :].astype(jnp.int32).astype(f32)
        unit = jnp.exp2(rest[0:NODES] * (1.0 / STEPS)) * (1.0 / TOP)
        left = left + scaled.reshape(NODES, OUTPUTS, LANES) * unit[:, None, :]
        left_hess = left_hess + (
            rest[NODES : 2 * NODES] * HESS_SPLIT + rest[2 * NODES : 3 * NODES]
        ) * (1.0 / HESS_UNIT)
    whole = left[:, :, LANES - 1 :]
    whole_hess = left_hess[:, LANES - 1 :]
    right = whole - left
    right_hess = whole_hess - left_hess

    def part_score(sums, hess):
        return jnp.sum(sums * sums, axis=1) / (hess + ridge_term)

    terms = part_score(left, left_hess) + part_score(right, right_hess)
    gain = (0.5 / OUTPUTS) * (terms - part_score(whole, whole_hess))
    for f in range(OWNED):
        for n in range(NODES):
            gain_out[f : f + 1, n * BINS : (n + 1) * BINS] = gain[
                n : n + 1, f * BINS : (f + 1) * BINS
            ]
    best = jnp.max(gain, axis=1, keepdims=True)
    sublane = lax.broadcasted_iota(jnp.int32, (NODES, 128), 0)
    lane = lax.broadcasted_iota(jnp.int32, (NODES, 128), 1)
    turned = jnp.max(jnp.where(sublane == lane, best, -jnp.inf), axis=0, keepdims=True)
    best_out[...] = jnp.broadcast_to(turned[:, 0:NODES], (devices, NODES))


def final_scores(parts, devices):
    return pl.pallas_call(
        functools.partial(score_kernel, devices),
        out_shape=(
            jax.ShapeDtypeStruct((OWNED, NODES * BINS), f32),
            jax.ShapeDtypeStruct((devices, NODES), f32),
        ),
        compiler_params=pltpu.CompilerParams(vmem_limit_bytes=48 << 20),
        name="split_scores",
    )(*parts)


def on_device(bin_index, gradient, hessian, row_node):
    swap = [(0, 1), (1, 0)]
    pay = payload(gradient, hessian, row_node, lax.axis_size(NEAR))
    pay = lax.all_to_all(pay, NEAR, 0, 0, tiled=True)
    pieces = list(cut_by_neighbour(bin_index))
    pieces[1] = lax.ppermute(pieces[1], "zl", swap)
    pieces[2] = lax.ppermute(pieces[2], "xh", swap)
    pieces[3] = lax.ppermute(pieces[3], ("xh", "zl"), [(0, 3), (1, 2), (2, 1), (3, 0)])
    leaving, kept = (2, 1, 3), (0,)
    near = [None, local_sums(1, (0,), leaving + kept, pay, pieces[:1])]
    near[1], pieces[1] = lax.optimization_barrier((near[1], pieces[1]))
    near[0] = local_sums(0, (0, 1), leaving, pay, pieces[:2])
    near, pieces[2:] = lax.optimization_barrier((near, pieces[2:]))
    theirs = local_sums(1, (1, 2, 3), leaving + kept, pay, pieces[1:], (near[1],))
    theirs = lax.ppermute(theirs, "c", swap)
    mine = local_sums(0, (2, 3), leaving, pay, pieces[2:], (near[0],))
    depth = lax.axis_size("zh")
    wires = to_wire(mine, theirs)
    wires, pay = lax.optimization_barrier((wires, pay))
    parts = [
        lax.ppermute(part, "zh", [(i, (i + d) % depth) for i in range(depth)])
        for d, part in zip(leaving, wires)
    ]
    parts = [local_sums(0, (0, 1, 2, 3), kept, pay, pieces), theirs] + parts
    gain, best = final_scores(parts, lax.axis_size(ALL))
    best = lax.all_to_all(best, ALL, 0, 0, tiled=True)
    return gain, jnp.max(best, axis=0)


def solution(mesh):
    split = Mesh(mesh.devices.reshape(2, 4, 2, 2, 4, 2), ALL)
    in_specs = (P(FEAT, ROW), P(None, ROW + FEAT), P(ROW + FEAT), P(ROW))
    out_specs = (P(FEAT + ROW, None), P())
    return jax.shard_map(
        on_device, mesh=split, in_specs=in_specs, out_specs=out_specs, check_vma=False
    )
```

```python
import functools

import jax
import jax.numpy as jnp
from jax import lax
from jax.experimental import pallas as pl
from jax.experimental.pallas import tpu as pltpu
from jax.sharding import Mesh
from jax.sharding import PartitionSpec as P

BINS = 64
NODES = 8
OUTPUTS = 32
OWNED = 4
LANES = OWNED * BINS
DEPTH = 256
GRAD_ROWS = NODES * OUTPUTS
SUM_ROWS = GRAD_ROWS + NODES
WIRE_ROWS = GRAD_ROWS + 4 * NODES
STEPS = 8.0
TOP = 32000.0
HESS_UNIT = 512.0
HESS_SPLIT = 4096.0
ROW = ("xh", "zh", "zl", "c")
FEAT = ("y", "xl")
ALL = ROW + FEAT
NEAR = ("xh", "zl", "y", "xl")
f32 = jnp.float32
bf16 = jnp.bfloat16

ridge_term = 1.0


def pay_kernel(grad_hbm, hess_hbm, nodes_hbm, pay, grad, hess, nodes, sems):
    copies = [
        pltpu.make_async_copy(src, dst, sems.at[i])
        for i, (src, dst) in enumerate(
            ((grad_hbm, grad), (hess_hbm, hess), (nodes_hbm, nodes))
        )
    ]
    for copy in copies:
        copy.start()
    for copy in copies:
        copy.wait()
    column = lax.axis_index(FEAT)
    blocks = grad.shape[1] // 128
    node = nodes[0:blocks, :]
    for s in range(1, nodes.shape[0] // blocks):
        node = jnp.where(column == s, nodes[s * blocks : (s + 1) * blocks, :], node)
    rest = jnp.concatenate(
        [
            hess[...].astype(f32),
            node.astype(f32),
            jnp.zeros((pay.shape[1] - (OUTPUTS + 2) * blocks, 128), f32),
        ],
        axis=0,
    ).astype(bf16)
    grads = [grad[:, 128 * i : 128 * (i + 1)] for i in range(blocks)]
    for s in range(pay.shape[0]):
        for i in range(blocks):
            pay[s, OUTPUTS * i : OUTPUTS * (i + 1), :] = grads[i]
        pay[s, OUTPUTS * blocks :, :] = rest


def payload(gradient, hessian, row_node, near):
    blocks = gradient.shape[1] // 128
    pay_rows = OUTPUTS * blocks + -(-2 * blocks // 8) * 8
    hessian = hessian.reshape(blocks, 128)
    row_node = row_node.reshape(-1, 128)
    return pl.pallas_call(
        pay_kernel,
        out_shape=jax.ShapeDtypeStruct((near, pay_rows, 128), bf16),
        in_specs=[pl.BlockSpec(memory_space=pl.ANY)] * 3,
        scratch_shapes=[
            pltpu.VMEM(gradient.shape, bf16),
            pltpu.VMEM(hessian.shape, bf16),
            pltpu.VMEM(row_node.shape, jnp.int32),
            pltpu.SemaphoreType.DMA((3,)),
        ],
        name="payload",
    )(gradient, hessian, row_node)


def cut_kernel(bins_hbm, p0, p1, p2, p3, bins, sems):
    xh, zl, c = lax.axis_index("xh"), lax.axis_index("zl"), lax.axis_index("c")
    tile = 2 * OWNED
    part = bins.shape[0] // sems.shape[0]
    copies = [
        pltpu.make_async_copy(
            bins_hbm.at[i * part : (i + 1) * part], bins.at[i * part : (i + 1) * part], sems.at[i]
        )
        for i in range(sems.shape[0])
    ]
    for copy in copies:
        copy.start()
    for copy in copies:
        copy.wait()
    depth = p0.shape[1]
    for r, out in enumerate((p0, p1, p2, p3)):
        for j in range(depth):
            t = ((xh ^ (r // 2)) * depth + j) * 2 + (zl ^ (r % 2))
            both = bins[pl.ds(pl.multiple_of(t * tile, tile), tile), :].astype(f32)
            first, second = both[0:OWNED], both[OWNED:tile]
            out[0, j] = jnp.where(c == 0, first, second).astype(bf16)
            out[1, j] = jnp.where(c == 0, second, first).astype(bf16)


def cut_by_neighbour(bin_index):
    features, shard_rows = bin_index.shape
    shape = jax.ShapeDtypeStruct((2, features // (8 * OWNED), OWNED, shard_rows), bf16)
    return pl.pallas_call(
        cut_kernel,
        out_shape=(shape,) * 4,
        in_specs=[pl.BlockSpec(memory_space=pl.ANY)],
        scratch_shapes=[
            pltpu.VMEM(bin_index.shape, jnp.int32),
            pltpu.SemaphoreType.DMA((4,)),
        ],
        compiler_params=pltpu.CompilerParams(vmem_limit_bytes=32 << 20),
        name="cut_bins",
    )(bin_index)


def sums_kernel(places, order, pay, *refs):
    pieces, before, out = refs[: len(places)], refs[len(places) : -1], refs[-1]
    pairs = len(order) // 2
    zh, depth = lax.axis_index("zh"), pieces[0].shape[1]
    columns = pay.shape[0] // 4
    layers = pay.shape[1] // OUTPUTS
    tiles = pieces[0].shape[-1] // DEPTH
    xh, zl = lax.axis_index("xh"), lax.axis_index("zl")

    def body(*sums):
        level = lax.broadcasted_iota(jnp.int32, (BINS, DEPTH), 0).astype(f32).astype(bf16)
        node_of_row = lax.broadcasted_iota(jnp.int32, (16, 128), 0).astype(f32).astype(bf16)
        one, zero = jnp.array(1, bf16), jnp.array(0, bf16)

        def by_node(group, layer):
            shard, i = group * columns + layer // layers, layer % layers
            grad = pay[shard, OUTPUTS * i : OUTPUTS * (i + 1), :]
            i = OUTPUTS * layers + i
            hess = jnp.broadcast_to(pay[shard, i : i + 1, :], (16, 128))
            i = i + layers
            node = jnp.broadcast_to(pay[shard, i : i + 1, :], (16, 128))
            rows = []
            for n in range(NODES):
                here = node == jnp.array(n, bf16)
                rows += [jnp.where(here, grad[k : k + 16], zero) for k in range(0, OUTPUTS, 16)]
            rows.append(jnp.where(node == node_of_row, hess, zero))
            return jnp.concatenate(rows, axis=0)

        def upto(bins):
            return jnp.concatenate(
                [
                    jnp.where(jnp.broadcast_to(bins[f : f + 1], (BINS, DEPTH)) <= level, one, zero)
                    for f in range(OWNED)
                ],
                axis=0,
            )

        for r, piece in zip(places, pieces):
            group = (xh ^ (r // 2)) * 2 + (zl ^ (r % 2))
            for t in range(tiles):
                values = jnp.concatenate(
                    [by_node(group, t * (DEPTH // 128) + k) for k in range(DEPTH // 128)], axis=1
                )
                def push(block, slot, m, piece=piece, t=t):
                    bins = piece[0, (zh + order[block]) % depth, :, t * DEPTH : (t + 1) * DEPTH]
                    pltpu.matmul_push_rhs(upto(bins), slot, m, transpose=True)

                for pair in range(pairs):
                    for m in range(2):
                        push(2 * pair + m, pair % 2, m)
                    for m in range(2):
                        pltpu.matmul_acc_lhs(sums[2 * pair + m], values, load_staged_rhs=pair % 2)
                if len(order) % 2:
                    slot = 1 if pairs else t // 2 % 2
                    push(2 * pairs, slot, t % 2)
                    pltpu.matmul_acc_lhs(sums[2 * pairs + t % 2], values, load_staged_rhs=slot)
        totals = [pltpu.matmul_pop(ref)[0:SUM_ROWS] for ref in sums]
        if len(order) % 2:
            totals[-2:] = [totals[-2] + totals[-1]]
        for j, total in enumerate(totals):
            for term in before:
                total = total + term[j]
            out[j] = total

    count = len(order) + len(order) % 2
    pl.run_scoped(body, *[pltpu.ACC(j % 2)((GRAD_ROWS + 16, LANES), f32) for j in range(count)])


def local_sums(core, places, order, pay, pieces, before=()):
    halves, depth, owned, shard_rows = pieces[0].shape
    blocks = len(order)
    bins_spec = pl.BlockSpec((1, depth, owned, shard_rows), lambda j: (core, 0, 0, 0))
    pay_spec = pl.BlockSpec(pay.shape, lambda j: (0, 0, 0))
    flops = 2 * SUM_ROWS * len(places) * shard_rows * LANES * blocks
    return pl.pallas_call(
        functools.partial(sums_kernel, places, order),
        out_shape=jax.ShapeDtypeStruct((blocks, SUM_ROWS, LANES), f32),
        grid=(1,),
        in_specs=[pay_spec]
        + [bins_spec] * len(places)
        + [pl.BlockSpec((blocks, SUM_ROWS, LANES), lambda j: (0, 0, 0))] * len(before),
        out_specs=pl.BlockSpec((blocks, SUM_ROWS, LANES), lambda j: (0, 0, 0)),
        cost_estimate=pl.CostEstimate(flops=flops, bytes_accessed=1 << 21, transcendentals=0),
        compiler_params=pltpu.CompilerParams(vmem_limit_bytes=32 << 20),
        name="left_sums",
    )(pay, *pieces, *before)


def wire_kernel(mine, theirs, *outs):
    for j, out in enumerate(outs):
        sums = mine[j] + theirs[j]
        grads = sums[0:GRAD_ROWS].reshape(NODES, OUTPUTS, LANES)
        largest = jnp.max(jnp.abs(grads), axis=1)
        octave = jnp.ceil(jnp.log2(jnp.maximum(largest, 1e-30)) * STEPS + 0.01)
        factor = TOP * jnp.exp2(octave * (-1.0 / STEPS))
        scaled = jnp.floor(grads * factor[:, None, :] + 0.5).reshape(GRAD_ROWS, LANES)
        out[0:GRAD_ROWS, :] = scaled.astype(jnp.int32).astype(jnp.int16)
        units = sums[GRAD_ROWS:SUM_ROWS] * HESS_UNIT
        high = jnp.floor(units * (1.0 / HESS_SPLIT))
        low = units - high * HESS_SPLIT
        rest = jnp.concatenate([octave, high, low, jnp.zeros_like(low)], axis=0)
        out[GRAD_ROWS:WIRE_ROWS, :] = rest.astype(jnp.int32).astype(jnp.int16)


def to_wire(mine, theirs):
    return pl.pallas_call(
        wire_kernel,
        out_shape=(jax.ShapeDtypeStruct((WIRE_ROWS, LANES), jnp.int16),) * mine.shape[0],
        compiler_params=pltpu.CompilerParams(vmem_limit_bytes=24 << 20),
        name="to_wire",
    )(mine, theirs)


def score_kernel(devices, *refs):
    (mine, theirs), parts, (gain_out, best_out) = refs[:2], refs[2:-2], refs[-2:]
    kept = mine[0] + theirs[theirs.shape[0] - 1]
    left = kept[0:GRAD_ROWS].reshape(NODES, OUTPUTS, LANES)
    left_hess = kept[GRAD_ROWS:SUM_ROWS]
    for part in parts:
        scaled = part[0:GRAD_ROWS, :].astype(jnp.int32).astype(f32)
        rest = part[GRAD_ROWS:WIRE_ROWS, :].astype(jnp.int32).astype(f32)
        unit = jnp.exp2(rest[0:NODES] * (1.0 / STEPS)) * (1.0 / TOP)
        left = left + scaled.reshape(NODES, OUTPUTS, LANES) * unit[:, None, :]
        left_hess = left_hess + (
            rest[NODES : 2 * NODES] * HESS_SPLIT + rest[2 * NODES : 3 * NODES]
        ) * (1.0 / HESS_UNIT)
    whole = left[:, :, LANES - 1 :]
    whole_hess = left_hess[:, LANES - 1 :]
    right = whole - left
    right_hess = whole_hess - left_hess

    def part_score(sums, hess):
        return jnp.sum(sums * sums, axis=1) / (hess + ridge_term)

    terms = part_score(left, left_hess) + part_score(right, right_hess)
    gain = (0.5 / OUTPUTS) * (terms - part_score(whole, whole_hess))
    for f in range(OWNED):
        for n in range(NODES):
            gain_out[f : f + 1, n * BINS : (n + 1) * BINS] = gain[
                n : n + 1, f * BINS : (f + 1) * BINS
            ]
    best = jnp.max(gain, axis=1, keepdims=True)
    sublane = lax.broadcasted_iota(jnp.int32, (NODES, 128), 0)
    lane = lax.broadcasted_iota(jnp.int32, (NODES, 128), 1)
    turned = jnp.max(jnp.where(sublane == lane, best, -jnp.inf), axis=0, keepdims=True)
    best_out[...] = jnp.broadcast_to(turned[:, 0:NODES], (devices, NODES))


def final_scores(parts, devices):
    return pl.pallas_call(
        functools.partial(score_kernel, devices),
        out_shape=(
            jax.ShapeDtypeStruct((OWNED, NODES * BINS), f32),
            jax.ShapeDtypeStruct((devices, NODES), f32),
        ),
        compiler_params=pltpu.CompilerParams(vmem_limit_bytes=48 << 20),
        name="split_scores",
    )(*parts)


def on_device(bin_index, gradient, hessian, row_node):
    swap = [(0, 1), (1, 0)]
    pay = payload(gradient, hessian, row_node, lax.axis_size(NEAR))
    pay = lax.all_to_all(pay, NEAR, 0, 0, tiled=True)
    pieces = list(cut_by_neighbour(bin_index))
    pieces[1] = lax.ppermute(pieces[1], "zl", swap)
    pieces[2] = lax.ppermute(pieces[2], "xh", swap)
    pieces[3] = lax.ppermute(pieces[3], ("xh", "zl"), [(0, 3), (1, 2), (2, 1), (3, 0)])
    leaving, kept = (2, 1, 3), (0,)
    near = [None, local_sums(1, (0,), leaving + kept, pay, pieces[:1])]
    near[1], pieces[1] = lax.optimization_barrier((near[1], pieces[1]))
    near[0] = local_sums(0, (0, 1), leaving, pay, pieces[:2])
    near[1] = local_sums(1, (1,), leaving + kept, pay, pieces[1:2], (near[1],))
    near, pieces[2:] = lax.optimization_barrier((near, pieces[2:]))
    theirs = local_sums(1, (2, 3), leaving + kept, pay, pieces[2:], (near[1],))
    theirs = lax.ppermute(theirs, "c", swap)
    mine = local_sums(0, (2, 3), leaving, pay, pieces[2:], (near[0],))
    depth = lax.axis_size("zh")
    wires = to_wire(mine, theirs)
    wires, pay = lax.optimization_barrier((wires, pay))
    parts = [
        lax.ppermute(part, "zh", [(i, (i + d) % depth) for i in range(depth)])
        for d, part in zip(leaving, wires)
    ]
    parts = [local_sums(0, (0, 1, 2, 3), kept, pay, pieces), theirs] + parts
    gain, best = final_scores(parts, lax.axis_size(ALL))
    best = lax.all_to_all(best, ALL, 0, 0, tiled=True)
    return gain, jnp.max(best, axis=0)


def solution(mesh):
    split = Mesh(mesh.devices.reshape(2, 4, 2, 2, 4, 2), ALL)
    in_specs = (P(FEAT, ROW), P(None, ROW + FEAT), P(ROW + FEAT), P(ROW))
    out_specs = (P(FEAT + ROW, None), P())
    return jax.shard_map(
        on_device, mesh=split, in_specs=in_specs, out_specs=out_specs, check_vma=False
    )
```

```python
import functools

import jax
import jax.numpy as jnp
from jax import lax
from jax.experimental import pallas as pl
from jax.experimental.pallas import tpu as pltpu
from jax.sharding import Mesh
from jax.sharding import PartitionSpec as P

BINS = 64
NODES = 8
OUTPUTS = 32
OWNED = 4
LANES = OWNED * BINS
DEPTH = 256
GRAD_ROWS = NODES * OUTPUTS
SUM_ROWS = GRAD_ROWS + NODES
WIRE_ROWS = GRAD_ROWS + 4 * NODES
STEPS = 8.0
TOP = 32000.0
HESS_UNIT = 512.0
HESS_SPLIT = 4096.0
ROW = ("xh", "zh", "zl", "c")
FEAT = ("y", "xl")
ALL = ROW + FEAT
NEAR = ("xh", "zl", "y", "xl")
f32 = jnp.float32
bf16 = jnp.bfloat16

ridge_term = 1.0


def pay_kernel(grad_hbm, hess_hbm, nodes_hbm, pay, grad, hess, nodes, sems):
    copies = [
        pltpu.make_async_copy(src, dst, sems.at[i])
        for i, (src, dst) in enumerate(
            ((grad_hbm, grad), (hess_hbm, hess), (nodes_hbm, nodes))
        )
    ]
    for copy in copies:
        copy.start()
    for copy in copies:
        copy.wait()
    column = lax.axis_index(FEAT)
    blocks = grad.shape[1] // 128
    node = nodes[0:blocks, :]
    for s in range(1, nodes.shape[0] // blocks):
        node = jnp.where(column == s, nodes[s * blocks : (s + 1) * blocks, :], node)
    rest = jnp.concatenate(
        [
            hess[...].astype(f32),
            node.astype(f32),
            jnp.zeros((pay.shape[1] - (OUTPUTS + 2) * blocks, 128), f32),
        ],
        axis=0,
    ).astype(bf16)
    grads = [grad[:, 128 * i : 128 * (i + 1)] for i in range(blocks)]
    for s in range(pay.shape[0]):
        for i in range(blocks):
            pay[s, OUTPUTS * i : OUTPUTS * (i + 1), :] = grads[i]
        pay[s, OUTPUTS * blocks :, :] = rest


def payload(gradient, hessian, row_node, near):
    blocks = gradient.shape[1] // 128
    pay_rows = OUTPUTS * blocks + -(-2 * blocks // 8) * 8
    hessian = hessian.reshape(blocks, 128)
    row_node = row_node.reshape(-1, 128)
    return pl.pallas_call(
        pay_kernel,
        out_shape=jax.ShapeDtypeStruct((near, pay_rows, 128), bf16),
        in_specs=[pl.BlockSpec(memory_space=pl.ANY)] * 3,
        scratch_shapes=[
            pltpu.VMEM(gradient.shape, bf16),
            pltpu.VMEM(hessian.shape, bf16),
            pltpu.VMEM(row_node.shape, jnp.int32),
            pltpu.SemaphoreType.DMA((3,)),
        ],
        name="payload",
    )(gradient, hessian, row_node)


def cut_kernel(bins_hbm, p0, p1, p2, p3, bins, sems):
    xh, zl, c = lax.axis_index("xh"), lax.axis_index("zl"), lax.axis_index("c")
    tile = 2 * OWNED
    part = bins.shape[0] // sems.shape[0]
    copies = [
        pltpu.make_async_copy(
            bins_hbm.at[i * part : (i + 1) * part], bins.at[i * part : (i + 1) * part], sems.at[i]
        )
        for i in range(sems.shape[0])
    ]
    for copy in copies:
        copy.start()
    for copy in copies:
        copy.wait()
    depth = p0.shape[1]
    for r, out in enumerate((p0, p1, p2, p3)):
        for j in range(depth):
            t = ((xh ^ (r // 2)) * depth + j) * 2 + (zl ^ (r % 2))
            both = bins[pl.ds(pl.multiple_of(t * tile, tile), tile), :].astype(f32)
            first, second = both[0:OWNED], both[OWNED:tile]
            out[0, j] = jnp.where(c == 0, first, second).astype(bf16)
            out[1, j] = jnp.where(c == 0, second, first).astype(bf16)


def cut_by_neighbour(bin_index):
    features, shard_rows = bin_index.shape
    shape = jax.ShapeDtypeStruct((2, features // (8 * OWNED), OWNED, shard_rows), bf16)
    return pl.pallas_call(
        cut_kernel,
        out_shape=(shape,) * 4,
        in_specs=[pl.BlockSpec(memory_space=pl.ANY)],
        scratch_shapes=[
            pltpu.VMEM(bin_index.shape, jnp.int32),
            pltpu.SemaphoreType.DMA((4,)),
        ],
        compiler_params=pltpu.CompilerParams(vmem_limit_bytes=32 << 20),
        name="cut_bins",
    )(bin_index)


def sums_kernel(places, order, pay, *refs):
    pieces, before, out = refs[: len(places)], refs[len(places) : -1], refs[-1]
    pairs = len(order) // 2
    zh, depth = lax.axis_index("zh"), pieces[0].shape[1]
    columns = pay.shape[0] // 4
    layers = pay.shape[1] // OUTPUTS
    tiles = pieces[0].shape[-1] // DEPTH
    xh, zl = lax.axis_index("xh"), lax.axis_index("zl")

    def body(*sums):
        level = lax.broadcasted_iota(jnp.int32, (BINS, DEPTH), 0).astype(f32).astype(bf16)
        node_of_row = lax.broadcasted_iota(jnp.int32, (16, 128), 0).astype(f32).astype(bf16)
        one, zero = jnp.array(1, bf16), jnp.array(0, bf16)

        def by_node(group, layer):
            shard, i = group * columns + layer // layers, layer % layers
            grad = pay[shard, OUTPUTS * i : OUTPUTS * (i + 1), :]
            i = OUTPUTS * layers + i
            hess = jnp.broadcast_to(pay[shard, i : i + 1, :], (16, 128))
            i = i + layers
            node = jnp.broadcast_to(pay[shard, i : i + 1, :], (16, 128))
            rows = []
            for n in range(NODES):
                here = node == jnp.array(n, bf16)
                rows += [jnp.where(here, grad[k : k + 16], zero) for k in range(0, OUTPUTS, 16)]
            rows.append(jnp.where(node == node_of_row, hess, zero))
            return jnp.concatenate(rows, axis=0)

        def upto(bins):
            return jnp.concatenate(
                [
                    jnp.where(jnp.broadcast_to(bins[f : f + 1], (BINS, DEPTH)) <= level, one, zero)
                    for f in range(OWNED)
                ],
                axis=0,
            )

        for r, piece in zip(places, pieces):
            group = (xh ^ (r // 2)) * 2 + (zl ^ (r % 2))
            for t in range(tiles):
                values = jnp.concatenate(
                    [by_node(group, t * (DEPTH // 128) + k) for k in range(DEPTH // 128)], axis=1
                )
                def push(block, slot, m, piece=piece, t=t):
                    bins = piece[0, (zh + order[block]) % depth, :, t * DEPTH : (t + 1) * DEPTH]
                    pltpu.matmul_push_rhs(upto(bins), slot, m, transpose=True)

                for pair in range(pairs):
                    for m in range(2):
                        push(2 * pair + m, pair % 2, m)
                    for m in range(2):
                        pltpu.matmul_acc_lhs(sums[2 * pair + m], values, load_staged_rhs=pair % 2)
                if len(order) % 2:
                    slot = 1 if pairs else t // 2 % 2
                    push(2 * pairs, slot, t % 2)
                    pltpu.matmul_acc_lhs(sums[2 * pairs + t % 2], values, load_staged_rhs=slot)
        totals = [pltpu.matmul_pop(ref)[0:SUM_ROWS] for ref in sums]
        if len(order) % 2:
            totals[-2:] = [totals[-2] + totals[-1]]
        for j, total in enumerate(totals):
            for term in before:
                total = total + term[j]
            out[j] = total

    count = len(order) + len(order) % 2
    pl.run_scoped(body, *[pltpu.ACC(j % 2)((GRAD_ROWS + 16, LANES), f32) for j in range(count)])


def local_sums(core, places, order, pay, pieces, before=()):
    halves, depth, owned, shard_rows = pieces[0].shape
    blocks = len(order)
    bins_spec = pl.BlockSpec((1, depth, owned, shard_rows), lambda j: (core, 0, 0, 0))
    pay_spec = pl.BlockSpec(pay.shape, lambda j: (0, 0, 0))
    flops = 2 * SUM_ROWS * len(places) * shard_rows * LANES * blocks
    return pl.pallas_call(
        functools.partial(sums_kernel, places, order),
        out_shape=jax.ShapeDtypeStruct((blocks, SUM_ROWS, LANES), f32),
        grid=(1,),
        in_specs=[pay_spec]
        + [bins_spec] * len(places)
        + [pl.BlockSpec((blocks, SUM_ROWS, LANES), lambda j: (0, 0, 0))] * len(before),
        out_specs=pl.BlockSpec((blocks, SUM_ROWS, LANES), lambda j: (0, 0, 0)),
        cost_estimate=pl.CostEstimate(flops=flops, bytes_accessed=1 << 21, transcendentals=0),
        compiler_params=pltpu.CompilerParams(vmem_limit_bytes=32 << 20),
        name="left_sums",
    )(pay, *pieces, *before)


def wire_kernel(mine, theirs, *outs):
    for j, out in enumerate(outs):
        sums = mine[j] + theirs[j]
        grads = sums[0:GRAD_ROWS].reshape(NODES, OUTPUTS, LANES)
        largest = jnp.max(jnp.abs(grads), axis=1)
        octave = jnp.ceil(jnp.log2(jnp.maximum(largest, 1e-30)) * STEPS + 0.01)
        factor = TOP * jnp.exp2(octave * (-1.0 / STEPS))
        scaled = jnp.floor(grads * factor[:, None, :] + 0.5).reshape(GRAD_ROWS, LANES)
        out[0:GRAD_ROWS, :] = scaled.astype(jnp.int32).astype(jnp.int16)
        units = sums[GRAD_ROWS:SUM_ROWS] * HESS_UNIT
        high = jnp.floor(units * (1.0 / HESS_SPLIT))
        low = units - high * HESS_SPLIT
        rest = jnp.concatenate([octave, high, low, jnp.zeros_like(low)], axis=0)
        out[GRAD_ROWS:WIRE_ROWS, :] = rest.astype(jnp.int32).astype(jnp.int16)


def to_wire(mine, theirs):
    return pl.pallas_call(
        wire_kernel,
        out_shape=(jax.ShapeDtypeStruct((WIRE_ROWS, LANES), jnp.int16),) * mine.shape[0],
        compiler_params=pltpu.CompilerParams(vmem_limit_bytes=24 << 20),
        name="to_wire",
    )(mine, theirs)


def score_kernel(devices, *refs):
    (mine, theirs), parts, (gain_out, best_out) = refs[:2], refs[2:-2], refs[-2:]
    kept = mine[0] + theirs[theirs.shape[0] - 1]
    left = kept[0:GRAD_ROWS].reshape(NODES, OUTPUTS, LANES)
    left_hess = kept[GRAD_ROWS:SUM_ROWS]
    for part in parts:
        scaled = part[0:GRAD_ROWS, :].astype(jnp.int32).astype(f32)
        rest = part[GRAD_ROWS:WIRE_ROWS, :].astype(jnp.int32).astype(f32)
        unit = jnp.exp2(rest[0:NODES] * (1.0 / STEPS)) * (1.0 / TOP)
        left = left + scaled.reshape(NODES, OUTPUTS, LANES) * unit[:, None, :]
        left_hess = left_hess + (
            rest[NODES : 2 * NODES] * HESS_SPLIT + rest[2 * NODES : 3 * NODES]
        ) * (1.0 / HESS_UNIT)
    whole = left[:, :, LANES - 1 :]
    whole_hess = left_hess[:, LANES - 1 :]
    right = whole - left
    right_hess = whole_hess - left_hess

    def part_score(sums, hess):
        return jnp.sum(sums * sums, axis=1) / (hess + ridge_term)

    terms = part_score(left, left_hess) + part_score(right, right_hess)
    gain = (0.5 / OUTPUTS) * (terms - part_score(whole, whole_hess))
    for f in range(OWNED):
        for n in range(NODES):
            gain_out[f : f + 1, n * BINS : (n + 1) * BINS] = gain[
                n : n + 1, f * BINS : (f + 1) * BINS
            ]
    best = jnp.max(gain, axis=1, keepdims=True)
    sublane = lax.broadcasted_iota(jnp.int32, (NODES, 128), 0)
    lane = lax.broadcasted_iota(jnp.int32, (NODES, 128), 1)
    turned = jnp.max(jnp.where(sublane == lane, best, -jnp.inf), axis=0, keepdims=True)
    best_out[...] = jnp.broadcast_to(turned[:, 0:NODES], (devices, NODES))


def final_scores(parts, devices):
    return pl.pallas_call(
        functools.partial(score_kernel, devices),
        out_shape=(
            jax.ShapeDtypeStruct((OWNED, NODES * BINS), f32),
            jax.ShapeDtypeStruct((devices, NODES), f32),
        ),
        compiler_params=pltpu.CompilerParams(vmem_limit_bytes=48 << 20),
        name="split_scores",
    )(*parts)


def on_device(bin_index, gradient, hessian, row_node):
    swap = [(0, 1), (1, 0)]
    pay = payload(gradient, hessian, row_node, lax.axis_size(NEAR))
    pay = lax.all_to_all(pay, NEAR, 0, 0, tiled=True)
    pieces = list(cut_by_neighbour(bin_index))
    pieces[1] = lax.ppermute(pieces[1], "zl", swap)
    pieces[2] = lax.ppermute(pieces[2], "xh", swap)
    pieces[3] = lax.ppermute(pieces[3], ("xh", "zl"), [(0, 3), (1, 2), (2, 1), (3, 0)])
    leaving, kept = (2, 1, 3), (0,)
    near = [
        local_sums(0, (0,), leaving, pay, pieces[:1]),
        local_sums(1, (0,), leaving + kept, pay, pieces[:1]),
    ]
    near, pieces[1] = lax.optimization_barrier((near, pieces[1]))
    near = [
        local_sums(0, (1,), leaving, pay, pieces[1:2], (near[0],)),
        local_sums(1, (1,), leaving + kept, pay, pieces[1:2], (near[1],)),
    ]
    near, pieces[2:] = lax.optimization_barrier((near, pieces[2:]))
    theirs = local_sums(1, (2, 3), leaving + kept, pay, pieces[2:], (near[1],))
    theirs = lax.ppermute(theirs, "c", swap)
    mine = local_sums(0, (2, 3), leaving, pay, pieces[2:], (near[0],))
    depth = lax.axis_size("zh")
    wires = to_wire(mine, theirs)
    wires, pay = lax.optimization_barrier((wires, pay))
    parts = [
        lax.ppermute(part, "zh", [(i, (i + d) % depth) for i in range(depth)])
        for d, part in zip(leaving, wires)
    ]
    parts = [local_sums(0, (0, 1, 2, 3), kept, pay, pieces), theirs] + parts
    gain, best = final_scores(parts, lax.axis_size(ALL))
    best = lax.all_to_all(best, ALL, 0, 0, tiled=True)
    return gain, jnp.max(best, axis=0)


def solution(mesh):
    split = Mesh(mesh.devices.reshape(2, 4, 2, 2, 4, 2), ALL)
    in_specs = (P(FEAT, ROW), P(None, ROW + FEAT), P(ROW + FEAT), P(ROW))
    out_specs = (P(FEAT + ROW, None), P())
    return jax.shard_map(
        on_device, mesh=split, in_specs=in_specs, out_specs=out_specs, check_vma=False
    )
```
